32 devices in a mesh: gx: 4 (over y, x), gy: 8 (over z, core).
Axes of the slice: x: 2, y: 2, z: 4, core: 2. Of those that a mesh axis runs over, the one named last changes fastest.
Arguments:
- fields: float32 [4, 128, 64, 1024], P(None, None, 'gx', 'gy'), may hold values from -6 to 6
- courant: float32 [2, 128, 64, 1024], P(None, None, 'gx', 'gy'), may hold values from -0.3 to 0.3
- sun_columns: int32 [4, 8, 2048], P('gx', 'gy'), may hold values from -1 to 2047, as said below
- rad_w1: bfloat16 [512, 1024], replicated, may hold values from -0.25 to 0.25
- rad_b1: float32 [1024], replicated, may hold values from -3 to 3
- rad_w2: bfloat16 [1024, 1024], replicated, may hold values from -0.1875 to 0.1875
- rad_b2: float32 [1024], replicated, may hold values from -3 to 3
- rad_w3: bfloat16 [1024, 512], replicated, may hold values from -0.1875 to 0.1875
- segment_route: int32 [2, 4, 8, 1024], P(None, 'gx', 'gy'), may hold values from 0 to 1023, as said below
- regrid_weights: bfloat16 [4, 8, 16, 128, 128], P('gx', 'gy'), may hold values from 0 to 1, as said below
- chem_w1: bfloat16 [256, 1024], replicated, may hold values from -0.375 to 0.375
- chem_b1: float32 [1024], replicated, may hold values from -3 to 3
- chem_w2: bfloat16 [1024, 256], replicated, may hold values from -0.1875 to 0.1875
Outputs:
- fields_out: float32 [4, 128, 64, 1024], P(None, None, 'gx', 'gy')
- chem_tendency: bfloat16 [4, 8, 2048, 256], P('gx', 'gy')
The draws below stay inside these ranges and needn't reach their ends.
Inputs may be any that keep to these rules, and one draw needn't show every extreme that they name: `sun_columns`: in each tile the live entries come first and are distinct columns of the tile; the rest are -1. Counting a tile's sunlit blocks as its live entries divided by 128, rounded up, a tile and the tile with the same first index and second index 4 further (modulo 8) have exactly 16 sunlit blocks together. `segment_route`: entry 0 is the receiving tile, entry 1 the slot there. Every tile receives exactly 1024 segments, one in each slot; no tile receives more than 64 segments from one tile, and some tile receives exactly 64 from one tile. `regrid_weights`: entries are nonnegative and each row sums to one up to rounding.
All inputs are finite; a program needn't handle non-finite values.
Results may differ from the reference program's by a relative error of at most 0.0075.
Values may be sent and summed in bfloat16 or wider, within the bound.
A program may use at most 128 MiB of HBM per device.

```python
import jax
import jax.numpy as jnp
from jax import lax

LEV = 128
NF = 4
RAD_HID = 1024
CHEM_HID = 1024
BLOCK = 128
SEG = 2
STEPS = 2
RAD_IN = 512
CHEM_IN = 256
COLS = 2048
BLOCKS = 16
NSEG = 1024
TX = 4
TY = 8
CAP = 64
NLAT = 64
NLON = 1024


def draw_sun_columns(key, part):
    half_tiles = TY // 2
    key_low = jax.random.fold_in(key, 101)
    key_spare = jax.random.fold_in(key, 102)
    key_order = jax.random.fold_in(key, 103)
    low_blocks = jax.random.randint(key_low, (TX, half_tiles), 0, BLOCKS + 1)
    low_blocks = low_blocks.at[0, 0].set(BLOCKS)
    block_counts = jnp.concatenate([low_blocks, BLOCKS - low_blocks], axis=1)
    spare = jax.random.randint(key_spare, (TX, TY), 0, BLOCK)
    lit_count = jnp.where(block_counts > 0, block_counts * BLOCK - spare, 0)
    order_keys = jax.random.split(key_order, TX * TY)
    orders = jax.vmap(jax.random.permutation, in_axes=(0, None))(order_keys, COLS).reshape(TX, TY, COLS)
    slot_index = jnp.arange(COLS)
    return jnp.where(slot_index[None, None, :] < lit_count[:, :, None], orders, -1).astype(jnp.int32)


def draw_segment_route(key, part):
    tile_count = TX * TY
    multiset = jnp.arange(tile_count * CAP, dtype=jnp.int32) // CAP
    remaining = jax.random.permutation(jax.random.fold_in(key, 201), multiset[CAP:])
    offsets = jnp.concatenate([multiset[:CAP], remaining])[:NSEG]
    offsets = (offsets + jax.random.randint(jax.random.fold_in(key, 202), (), 0, tile_count)) % tile_count
    first_perm = jax.random.permutation(jax.random.fold_in(key, 203), tile_count)
    second_perm = jax.random.permutation(jax.random.fold_in(key, 204), tile_count)
    segment_perm = jax.random.permutation(jax.random.fold_in(key, 205), NSEG)
    slot_perm = jax.random.permutation(jax.random.fold_in(key, 206), NSEG)
    source_turn = jax.random.randint(jax.random.fold_in(key, 207), (tile_count,), 0, NSEG)
    target_turn = jax.random.randint(jax.random.fold_in(key, 208), (tile_count,), 0, NSEG)
    segment_index = jnp.arange(NSEG)
    inverse = jnp.argsort(segment_perm)
    which = inverse[(segment_index[None, :] - source_turn[:, None]) % NSEG]
    destination = second_perm[(first_perm[:, None] + offsets[which]) % tile_count]
    arrival = (slot_perm[which] + target_turn[destination]) % NSEG
    return jnp.stack([destination, arrival]).reshape(2, TX, TY, NSEG).astype(jnp.int32)


def draw_regrid_weights(key, part):
    shape = (TX, TY, BLOCKS, BLOCK, BLOCK)
    raw_weights = jax.random.uniform(key, shape, jnp.float32, 0.0, 1.0)
    raw_weights = raw_weights + 0.5 * BLOCK * jnp.eye(BLOCK, dtype=jnp.float32)
    return (raw_weights / jnp.sum(raw_weights, axis=-1, keepdims=True)).astype(jnp.bfloat16)


def block_levels(own_key, dims, shards, low, high):
    factor_of, own = 1.0, jax.random.fold_in(own_key, 6)
    for axis_at, parts in shards:
        heights = jnp.exp(jax.random.uniform(jax.random.fold_in(own, axis_at), (parts,), jnp.float32, low / len(shards), high / len(shards)))
        factor_of = factor_of * jnp.repeat(heights, dims[axis_at] // parts).reshape([-1 if axis == axis_at else 1 for axis in range(len(dims))])
    return factor_of


def scatter_about(own_key, extent, scale, bound, cuts=(), kind=jnp.bfloat16):
    entries = scale * jax.random.normal(own_key, extent, jnp.float32)
    if cuts:
        entries = entries * block_levels(own_key, extent, cuts, -0.22, 0.18)
    return jnp.clip(entries, -bound, bound).astype(kind)


def setup_inputs(seed: int = 0) -> dict:
    key_list = jax.random.split(jax.random.key(seed), 14)
    fields = scatter_about(key_list[0], (NF, LEV, NLAT, NLON), 1.0, 6.0, ((2, 4), (3, 8)), jnp.float32)
    courant = jnp.clip(jax.random.uniform(key_list[1], (2, LEV, NLAT, NLON), jnp.float32, -0.3, 0.3) * block_levels(key_list[1], (2, LEV, NLAT, NLON), ((2, 4), (3, 8)), -0.4, 0.0), -0.3, 0.3)
    sun_columns = draw_sun_columns(jax.random.fold_in(key_list[13], 71), 0)
    rad_w1 = scatter_about(key_list[3], (RAD_IN, RAD_HID), RAD_IN ** -0.5, 0.25)
    rad_b1 = scatter_about(key_list[4], (RAD_HID,), 0.5, 3.0, (), jnp.float32)
    rad_w2 = scatter_about(key_list[5], (RAD_HID, RAD_HID), RAD_HID ** -0.5, 0.1875)
    rad_b2 = scatter_about(key_list[6], (RAD_HID,), 0.5, 3.0, (), jnp.float32)
    rad_w3 = scatter_about(key_list[7], (RAD_HID, RAD_IN), RAD_HID ** -0.5, 0.1875)
    segment_route = draw_segment_route(jax.random.fold_in(key_list[13], 71), 0)
    regrid_weights = draw_regrid_weights(jax.random.fold_in(key_list[13], 71), 0)
    chem_w1 = scatter_about(key_list[10], (CHEM_IN, CHEM_HID), CHEM_IN ** -0.5, 0.375)
    chem_b1 = scatter_about(key_list[11], (CHEM_HID,), 0.5, 3.0, (), jnp.float32)
    chem_w2 = scatter_about(key_list[12], (CHEM_HID, CHEM_IN), CHEM_HID ** -0.5, 0.1875)
    return {"fields": fields, "courant": courant, "sun_columns": sun_columns, "rad_w1": rad_w1, "rad_b1": rad_b1, "rad_w2": rad_w2, "rad_b2": rad_b2, "rad_w3": rad_w3, "segment_route": segment_route, "regrid_weights": regrid_weights, "chem_w1": chem_w1, "chem_b1": chem_b1, "chem_w2": chem_w2}


def advect(fields, courant):
    lat_count = fields.shape[2]
    cells_lat = jnp.pad(fields, ((0, 0), (0, 0), (1, 1), (0, 0)))
    speed_lat = jnp.pad(courant[0], ((0, 0), (1, 1), (0, 0)))
    lower_row = jnp.arange(lat_count + 1) - 1
    valid_face = ((lower_row >= 0) & (lower_row <= lat_count - 2)).astype(jnp.float32)
    face_lat = 0.5 * (speed_lat[:, :-1] + speed_lat[:, 1:]) * valid_face[None, :, None]
    flux_lat = jnp.maximum(face_lat, 0.0) * cells_lat[:, :, :-1] + jnp.minimum(face_lat, 0.0) * cells_lat[:, :, 1:]
    cells_lon = jnp.pad(fields, ((0, 0), (0, 0), (0, 0), (1, 1)), mode="wrap")
    speed_lon = jnp.pad(courant[1], ((0, 0), (0, 0), (1, 1)), mode="wrap")
    face_lon = 0.5 * (speed_lon[:, :, :-1] + speed_lon[:, :, 1:])
    flux_lon = jnp.maximum(face_lon, 0.0) * cells_lon[..., :-1] + jnp.minimum(face_lon, 0.0) * cells_lon[..., 1:]
    return fields - (flux_lat[:, :, 1:] - flux_lat[:, :, :-1]) - (flux_lon[..., 1:] - flux_lon[..., :-1])


def radiation_net(features, rad_w1, rad_b1, rad_w2, rad_b2, rad_w3):
    contract = (((0,), (0,)), ((), ()))
    layer_one = jax.nn.silu(lax.dot_general(rad_w1, features, contract, preferred_element_type=jnp.float32) + rad_b1[:, None]).astype(jnp.bfloat16)
    layer_two = jax.nn.silu(lax.dot_general(rad_w2, layer_one, contract, preferred_element_type=jnp.float32) + rad_b2[:, None]).astype(jnp.bfloat16)
    return lax.dot_general(rad_w3, layer_two, contract, preferred_element_type=jnp.float32)


def radiate(fields, sun_columns, rad_w1, rad_b1, rad_w2, rad_b2, rad_w3):
    field_count, levels, lat_count, lon_count = fields.shape
    tile_rows = lat_count // TX
    tile_cols = lon_count // TY
    tiled = fields.reshape(field_count * levels, TX, tile_rows, TY, tile_cols)
    tiled = tiled.transpose(1, 3, 0, 2, 4).reshape(TX * TY, field_count * levels, tile_rows * tile_cols)

    def one_tile(tile_pair):
        tile_fields, slot_list = tile_pair
        lit_mask = slot_list >= 0
        safe_index = jnp.where(lit_mask, slot_list, 0).astype(jnp.int32)
        features = (jnp.take(tile_fields, safe_index, axis=1) * lit_mask[None, :]).astype(jnp.bfloat16)
        heating = radiation_net(features, rad_w1, rad_b1, rad_w2, rad_b2, rad_w3)
        return jnp.zeros_like(tile_fields).at[:, safe_index].add(jnp.where(lit_mask[None, :], heating, 0.0))

    tendency = lax.map(one_tile, (tiled, sun_columns.reshape(TX * TY, -1)))
    tendency = tendency.reshape(TX, TY, field_count * levels, tile_rows, tile_cols).transpose(2, 0, 3, 1, 4)
    return fields + tendency.reshape(fields.shape)


def chemistry(fields, segment_route, regrid_weights, chem_w1, chem_b1, chem_w2):
    levels = fields.shape[1]
    tile_rows = fields.shape[2] // TX
    tile_cols = fields.shape[3] // TY
    source = fields[2:4].astype(jnp.bfloat16)
    tiled = source.reshape(2 * levels, TX, tile_rows, TY, tile_cols).transpose(1, 3, 2, 4, 0)
    tiled = tiled.reshape(TX * TY * NSEG, SEG, 2 * levels)
    placed = jnp.zeros((TX * TY, NSEG, SEG, 2 * levels), jnp.bfloat16)
    placed = placed.at[segment_route[0].reshape(-1).astype(jnp.int32), segment_route[1].reshape(-1).astype(jnp.int32)].set(tiled)
    chem_cells = placed.reshape(TX * TY, BLOCKS, BLOCK, 2 * levels)
    mixing = regrid_weights.reshape(TX * TY, BLOCKS, BLOCK, BLOCK)
    regridded = jnp.einsum("tjab,tjbf->tjaf", mixing.astype(jnp.float32), chem_cells.astype(jnp.float32)).astype(jnp.bfloat16)
    flat_cells = regridded.reshape(-1, 2 * levels)
    chem_hidden = jax.nn.silu(jnp.dot(flat_cells, chem_w1, preferred_element_type=jnp.float32) + chem_b1).astype(jnp.bfloat16)
    output = jnp.dot(chem_hidden, chem_w2, preferred_element_type=jnp.float32).astype(jnp.bfloat16)
    return output.reshape(TX, TY, tile_rows * tile_cols, 2 * levels)


def reference(fields, courant, sun_columns, rad_w1, rad_b1, rad_w2, rad_b2, rad_w3, segment_route, regrid_weights, chem_w1, chem_b1, chem_w2):
    current = fields
    for repeat in range(STEPS):
        current = advect(current, courant)
        current = radiate(current, sun_columns, rad_w1, rad_b1, rad_w2, rad_b2, rad_w3)
    chem_output = chemistry(current, segment_route, regrid_weights, chem_w1, chem_b1, chem_w2)
    return current, chem_output
```

```python
import functools

import jax
import jax.numpy as jnp
from jax import lax
from jax.experimental import pallas as pl
from jax.experimental.pallas import tpu as pltpu
from jax.sharding import PartitionSpec as P

BLOCK = 128
SEG = 2
STEPS = 2
GROUP = 2
VMEM = pl.BlockSpec(memory_space=pltpu.VMEM)
SMEM = pl.BlockSpec(memory_space=pltpu.SMEM)


def silu(x):
    half = 0.5 * x
    return half + half * jnp.tanh(half)


def lanes_of(shape):
    return lax.broadcasted_iota(jnp.int32, shape, len(shape) - 1)


def prep_kernel(rows, f_ref, c_ref, v_ref, lat_ref, lon_ref, edge_ref, cedge_ref):
    total = f_ref.shape[0] // rows
    levels = lat_ref.shape[1]
    width = f_ref.shape[1]
    edge_ref[...] = jnp.zeros_like(edge_ref)
    cedge_ref[...] = jnp.zeros_like(cedge_ref)

    def edges(ref, value, r):
        lane = lanes_of(value.shape)
        ref[...] = jnp.where(
            lane == r,
            pltpu.roll(value, r, axis=1),
            jnp.where(lane == rows + r, pltpu.roll(value, rows + 1 + r, axis=1), ref[...]),
        )

    def body(r, carry):
        value = f_ref[pl.ds(r, total, stride=rows), :]
        v_ref[r] = value
        edges(edge_ref, value, r)
        lat_ref[r] = c_ref[pl.ds(r, levels, stride=rows), :]
        lon = c_ref[pl.ds(levels * rows + r, levels, stride=rows), :]
        lon_ref[r] = lon
        edges(cedge_ref, lon, r)
        return carry

    lax.fori_loop(0, rows, body, 0)


def prep(fields, courant):
    count, levels, rows, cols = fields.shape
    total = count * levels
    f32 = jnp.float32
    return pl.pallas_call(
        functools.partial(prep_kernel, rows),
        out_shape=(
            jax.ShapeDtypeStruct((rows, total, cols), f32),
            jax.ShapeDtypeStruct((rows, levels, cols), f32),
            jax.ShapeDtypeStruct((rows, levels, cols), f32),
            jax.ShapeDtypeStruct((total, cols), f32),
            jax.ShapeDtypeStruct((levels, cols), f32),
        ),
        in_specs=[VMEM, VMEM],
        out_specs=(VMEM,) * 5,
        name="prep",
    )(fields.reshape(total * rows, cols), courant.reshape(2 * levels * rows, cols))


def step_kernel(
    last,
    flag_ref,
    v_ref,
    lat_ref,
    lon_ref,
    north_ref,
    south_ref,
    west_ref,
    east_ref,
    cnorth_ref,
    csouth_ref,
    cwest_ref,
    ceast_ref,
    lit_ref,
    w1_ref,
    b1_ref,
    w2_ref,
    b2_ref,
    w3_ref,
    *refs,
):
    rows, total, width = v_ref.shape
    levels = lat_ref.shape[1]
    count = total // levels
    if last:
        out_ref, src_ref, adv_ref, x_ref, one_ref, two_ref = refs
    else:
        out_ref, edge_ref, adv_ref, x_ref, one_ref, two_ref = refs
        edge_ref[...] = jnp.zeros_like(edge_ref)
    hidden = w1_ref.shape[0]
    lane = lanes_of((levels, width))

    def advect_row(r, slot):
        is_top = r == 0
        is_low = r == rows - 1
        up = jnp.maximum(r - 1, 0)
        down = jnp.minimum(r + 1, rows - 1)
        here = lat_ref[r]
        above = jnp.where(is_top, cnorth_ref[...], lat_ref[up])
        below = jnp.where(is_low, csouth_ref[...], lat_ref[down])
        face0 = 0.5 * (above + here) * jnp.where(is_top, flag_ref[0], 1.0)
        face1 = 0.5 * (here + below) * jnp.where(is_low, flag_ref[1], 1.0)
        pos0, neg0 = jnp.maximum(face0, 0.0), jnp.minimum(face0, 0.0)
        pos1, neg1 = jnp.maximum(face1, 0.0), jnp.minimum(face1, 0.0)

        def west_of(value, halo):
            return jnp.where(
                lane == 0, pltpu.roll(halo, width - rows - r, axis=1), pltpu.roll(value, 1, axis=1)
            )

        def east_of(value, halo):
            return jnp.where(
                lane == width - 1,
                pltpu.roll(halo, width - 1 - r, axis=1),
                pltpu.roll(value, width - 1, axis=1),
            )

        c = lon_ref[r]
        g0 = 0.5 * (west_of(c, cwest_ref[...]) + c)
        g1 = 0.5 * (c + east_of(c, ceast_ref[...]))
        gpos0, gneg0 = jnp.maximum(g0, 0.0), jnp.minimum(g0, 0.0)
        gpos1, gneg1 = jnp.maximum(g1, 0.0), jnp.minimum(g1, 0.0)
        for f in range(count):
            part = slice(f * levels, (f + 1) * levels)
            v = v_ref[r, part, :]
            vn = jnp.where(is_top, north_ref[part, :], v_ref[up, part, :])
            vs = jnp.where(is_low, south_ref[part, :], v_ref[down, part, :])
            vw = west_of(v, west_ref[part, :])
            ve = east_of(v, east_ref[part, :])
            f0 = pos0 * vn + neg0 * v
            f1 = pos1 * v + neg1 * vs
            h0 = gpos0 * vw + gneg0 * v
            h1 = gpos1 * v + gneg1 * ve
            new = v - (f1 - f0) - (h1 - h0)
            adv_ref[part, slot * width : (slot + 1) * width] = new
            x_ref[part, slot * width : (slot + 1) * width] = new.astype(jnp.bfloat16)

    def body(i, carry):
        for k in range(GROUP):
            advect_row(i * GROUP + k, k)
        chunk = 256
        for h in range(0, hidden, chunk):
            acc = jnp.dot(w1_ref[h : h + chunk, :], x_ref[...], preferred_element_type=jnp.float32)
            bias = jnp.concatenate([b1_ref[h : h + chunk, :]] * GROUP, axis=1)
            one_ref[h : h + chunk, :] = silu(acc + bias).astype(jnp.bfloat16)
        for h in range(0, hidden, chunk):
            acc = jnp.dot(w2_ref[h : h + chunk, :], one_ref[...], preferred_element_type=jnp.float32)
            bias = jnp.concatenate([b2_ref[h : h + chunk, :]] * GROUP, axis=1)
            two_ref[h : h + chunk, :] = silu(acc + bias).astype(jnp.bfloat16)
        lit = jnp.concatenate([lit_ref[i * GROUP + k] for k in range(GROUP)], axis=1)
        for h in range(0, total, chunk):
            heat = jnp.dot(w3_ref[h : h + chunk, :], two_ref[...], preferred_element_type=jnp.float32)
            new = adv_ref[h : h + chunk, :] + jnp.where(lit > 0.0, heat, 0.0)
            for k in range(GROUP):
                r = i * GROUP + k
                piece = new[:, k * width : (k + 1) * width]
                if last:
                    out_ref[pl.ds(h * rows + r, chunk, stride=rows), :] = piece
                    if h >= 2 * levels:
                        src_ref[
                            h - 2 * levels : h - 2 * levels + chunk,
                            pl.ds(pl.multiple_of(r * width, width), width),
                        ] = piece.astype(jnp.bfloat16)
                else:
                    out_ref[r, h : h + chunk, :] = piece
                    at = lanes_of(piece.shape)
                    edge_ref[h : h + chunk, :] = jnp.where(
                        at == r,
                        pltpu.roll(piece, r, axis=1),
                        jnp.where(
                            at == rows + r,
                            pltpu.roll(piece, rows + 1 + r, axis=1),
                            edge_ref[h : h + chunk, :],
                        ),
                    )
        return carry

    lax.fori_loop(0, rows // GROUP, body, 0)


def step(last, flags, v, lat, lon, halos, chalos, lit, nets):
    rows, total, cols = v.shape
    levels = lat.shape[1]
    hidden = nets[0].shape[0]
    f32, bf16 = jnp.float32, jnp.bfloat16
    if last:
        outs = (
            jax.ShapeDtypeStruct((total * rows, cols), f32),
            jax.ShapeDtypeStruct((2 * levels, rows * cols), bf16),
        )
    else:
        outs = (
            jax.ShapeDtypeStruct((rows, total, cols), f32),
            jax.ShapeDtypeStruct((total, cols), f32),
        )
    wide = GROUP * cols
    return pl.pallas_call(
        functools.partial(step_kernel, last),
        out_shape=outs,
        in_specs=[SMEM] + [VMEM] * 17,
        out_specs=(VMEM,) * 2,
        scratch_shapes=[
            pltpu.VMEM((total, wide), f32),
            pltpu.VMEM((total, wide), bf16),
            pltpu.VMEM((hidden, wide), bf16),
            pltpu.VMEM((hidden, wide), bf16),
        ],
        name="step_last" if last else "step_first",
    )(flags, v, lat, lon, *halos, *chalos, lit, *nets)


def pack_kernel(source_ref, target_ref, out_ref):
    tile = out_ref.shape[0]
    feats, cols = source_ref.shape
    slot = lax.broadcasted_iota(jnp.int32, (tile, cols), 0) + pl.program_id(0) * tile
    lane = lanes_of((tile, cols))
    match = slot == target_ref[...]
    for c in range(SEG):
        hit = (match & (lane % SEG == c)).astype(jnp.float32).astype(jnp.bfloat16)
        out_ref[:, c * feats : (c + 1) * feats] = lax.dot_general(
            hit, source_ref[...], (((1,), (1,)), ((), ())), preferred_element_type=jnp.float32
        ).astype(jnp.bfloat16)


def pack(source, target, slots):
    feats, cols = source.shape
    tile = 256
    return pl.pallas_call(
        pack_kernel,
        grid=(slots // tile,),
        out_shape=jax.ShapeDtypeStruct((slots, SEG * feats), jnp.bfloat16),
        in_specs=[
            pl.BlockSpec((feats, cols), lambda i: (0, 0)),
            pl.BlockSpec((1, cols), lambda i: (0, 0)),
        ],
        out_specs=pl.BlockSpec((tile, SEG * feats), lambda i: (i, 0)),
        name="pack",
    )(source, target)


def chem_kernel(arrived_ref, tag_ref, regrid_ref, w1_ref, b1_ref, w2_ref, out_ref, cell_ref):
    slots = arrived_ref.shape[0]
    feats = arrived_ref.shape[1] // SEG
    cells = out_ref.shape[0]
    segs = cells // SEG
    f32, bf16 = jnp.float32, jnp.bfloat16
    seg = lax.broadcasted_iota(jnp.int32, (segs, slots), 0) + pl.program_id(0) * segs
    pick = (seg == tag_ref[...]).astype(f32).astype(bf16)
    placed = jnp.dot(pick, arrived_ref[...], preferred_element_type=f32).astype(bf16)
    half = BLOCK // SEG
    row = lax.broadcasted_iota(jnp.int32, (BLOCK, BLOCK), 0)
    col = lax.broadcasted_iota(jnp.int32, (BLOCK, BLOCK), 1)
    order = (row == (col % half) * SEG + col // half).astype(f32).astype(bf16)
    for j in range(cells // BLOCK):
        mix = jnp.dot(regrid_ref[j], order, preferred_element_type=f32).astype(bf16)
        block = placed[j * half : (j + 1) * half, :]
        stacked = jnp.concatenate(
            [block[:, c * feats : (c + 1) * feats] for c in range(SEG)], axis=0
        )
        cell_ref[j * BLOCK : (j + 1) * BLOCK, :] = jnp.dot(
            mix, stacked, preferred_element_type=f32
        ).astype(bf16)
    hid = jnp.dot(cell_ref[...], w1_ref[...], preferred_element_type=f32) + b1_ref[...]
    out_ref[...] = jnp.dot(
        silu(hid).astype(bf16), w2_ref[...], preferred_element_type=f32
    ).astype(bf16)


def chem(arrived, tags, regrid, w1, b1, w2):
    slots, wide = arrived.shape
    feats = wide // SEG
    blocks = regrid.shape[0]
    per = 4
    hidden = w1.shape[1]
    whole = lambda *shape: pl.BlockSpec(shape, lambda i: (0,) * len(shape))
    return pl.pallas_call(
        chem_kernel,
        grid=(blocks // per,),
        out_shape=jax.ShapeDtypeStruct((blocks * BLOCK, feats), jnp.bfloat16),
        in_specs=[
            whole(slots, wide),
            whole(1, slots),
            pl.BlockSpec((per, BLOCK, BLOCK), lambda i: (i, 0, 0)),
            whole(feats, hidden),
            whole(1, hidden),
            whole(hidden, feats),
        ],
        out_specs=pl.BlockSpec((per * BLOCK, feats), lambda i: (i, 0)),
        scratch_shapes=[pltpu.VMEM((per * BLOCK, feats), jnp.bfloat16)],
        name="chem",
    )(arrived, tags, regrid, w1, b1, w2)


def shifted(axis, first, last, periodic):
    count = lax.axis_size(axis)
    forward = [(i, i + 1) for i in range(count - 1)]
    if periodic:
        forward.append((count - 1, 0))
    backward = [(target, source) for source, target in forward]
    return lax.ppermute(last, axis, forward), lax.ppermute(first, axis, backward)


def local(
    fields,
    courant,
    sun_columns,
    rad_w1,
    rad_b1,
    rad_w2,
    rad_b2,
    rad_w3,
    segment_route,
    regrid_weights,
    chem_w1,
    chem_b1,
    chem_w2,
):
    field_count, levels, rows, cols = fields.shape
    columns = rows * cols
    v, lat, lon, edge, cedge = prep(fields, courant)
    cwest, ceast = shifted("gy", cedge, cedge, True)
    cnorth, csouth = shifted("gx", lat[0], lat[rows - 1], False)

    place = lax.axis_index("gx")
    flags = jnp.stack([place > 0, place < lax.axis_size("gx") - 1]).astype(jnp.float32)
    slot_list = sun_columns.reshape(-1)
    lit = jnp.any(slot_list[:, None] == jnp.arange(columns)[None, :], axis=0)
    lit = lit.astype(jnp.float32).reshape(rows, 1, cols)

    def wide(bias):
        return jnp.broadcast_to(bias[:, None], (bias.shape[0], cols))

    nets = (rad_w1.T, wide(rad_b1), rad_w2.T, wide(rad_b2), rad_w3.T)

    segment_count = columns // SEG
    tile_count = lax.axis_size("gx") * lax.axis_size("gy")
    capacity = max(2, 2 * segment_count // tile_count)
    slots = tile_count * capacity
    destination = segment_route[0].reshape(-1)
    arrival_slot = segment_route[1].reshape(-1)
    segment_index = jnp.arange(segment_count)
    same_target = (destination[None, :] == destination[:, None]) & (
        segment_index[None, :] < segment_index[:, None]
    )
    order_rank = jnp.sum(same_target.astype(jnp.int32), axis=1)
    target_row = destination * capacity + order_rank
    placement = target_row[None, :] == jnp.arange(slots)[:, None]
    slot_tags = jnp.sum(jnp.where(placement, arrival_slot[None, :] + 1, 0), axis=1) - 1
    tags = lax.all_to_all(
        slot_tags.reshape(tile_count, capacity), ("gx", "gy"), split_axis=0, concat_axis=0, tiled=True
    ).reshape(1, slots)
    column_target = jnp.repeat(target_row, SEG).reshape(1, columns)

    for repeat in range(STEPS):
        last = repeat == STEPS - 1
        north, south = shifted("gx", v[0], v[rows - 1], False)
        west, east = shifted("gy", edge, edge, True)
        halos = (north, south, west, east)
        v, edge = step(last, flags, v, lat, lon, halos, (cnorth, csouth, cwest, ceast), lit, nets)
    source = edge
    packed = pack(source, column_target, slots).reshape(tile_count, capacity, SEG * 2 * levels)
    arrived = lax.all_to_all(packed, ("gx", "gy"), split_axis=0, concat_axis=0, tiled=True)
    arrived = arrived.reshape(slots, SEG * 2 * levels)
    output = chem(arrived, tags, regrid_weights[0, 0], chem_w1, chem_b1.reshape(1, -1), chem_w2)
    return (
        v.reshape(field_count, levels, rows, cols),
        output.reshape(1, 1, columns, 2 * levels),
    )


def solution(mesh):
    return jax.shard_map(
        local,
        mesh=mesh,
        in_specs=(
            P(None, None, "gx", "gy"),
            P(None, None, "gx", "gy"),
            P("gx", "gy", None),
            P(),
            P(),
            P(),
            P(),
            P(),
            P(None, "gx", "gy", None),
            P("gx", "gy", None, None, None),
            P(),
            P(),
            P(),
        ),
        out_specs=(P(None, None, "gx", "gy"), P("gx", "gy", None, None)),
        check_vma=False,
    )
```

```python
import functools

import jax
import jax.numpy as jnp
from jax import lax
from jax.experimental import pallas as pl
from jax.experimental.pallas import tpu as pltpu
from jax.sharding import PartitionSpec as P

BLOCK = 128
SEG = 2
STEPS = 2
GROUP = 2
VMEM = pl.BlockSpec(memory_space=pltpu.VMEM)
SMEM = pl.BlockSpec(memory_space=pltpu.SMEM)


def silu(x):
    half = 0.5 * x
    return half + half * jnp.tanh(half)


def lanes_of(shape):
    return lax.broadcasted_iota(jnp.int32, shape, len(shape) - 1)


def prep_kernel(rows, f_ref, c_ref, v_ref, lat_ref, lon_ref, rim_ref, edge_ref):
    total = f_ref.shape[0] // rows
    levels = lat_ref.shape[1]
    edge_ref[...] = jnp.zeros_like(edge_ref)

    def edges(part, value, r):
        lane = lanes_of(value.shape)
        edge_ref[part, :] = jnp.where(
            lane == r,
            pltpu.roll(value, r, axis=1),
            jnp.where(
                lane == rows + r, pltpu.roll(value, rows + 1 + r, axis=1), edge_ref[part, :]
            ),
        )

    def body(r, carry):
        value = f_ref[pl.ds(r, total, stride=rows), :]
        v_ref[r] = value
        edges(slice(0, total), value, r)
        lat_ref[r] = c_ref[pl.ds(r, levels, stride=rows), :]
        lon = c_ref[pl.ds(levels * rows + r, levels, stride=rows), :]
        lon_ref[r] = lon
        edges(slice(total, total + levels), lon, r)
        return carry

    lax.fori_loop(0, rows, body, 0)
    for k, r in enumerate((0, rows - 1)):
        rim_ref[k, :total, :] = v_ref[r].astype(jnp.bfloat16)
        rim_ref[k, total:, :] = lat_ref[r].astype(jnp.bfloat16)
    rim_ref[2] = edge_ref[...].astype(jnp.bfloat16)


def prep(fields, courant):
    count, levels, rows, cols = fields.shape
    total = count * levels
    f32 = jnp.float32
    return pl.pallas_call(
        functools.partial(prep_kernel, rows),
        out_shape=(
            jax.ShapeDtypeStruct((rows, total, cols), f32),
            jax.ShapeDtypeStruct((rows, levels, cols), f32),
            jax.ShapeDtypeStruct((rows, levels, cols), f32),
            jax.ShapeDtypeStruct((3, total + levels, cols), jnp.bfloat16),
        ),
        in_specs=[VMEM, VMEM],
        out_specs=(VMEM,) * 4,
        scratch_shapes=[pltpu.VMEM((total + levels, cols), f32)],
        name="prep",
    )(fields.reshape(total * rows, cols), courant.reshape(2 * levels * rows, cols))


def exchange_kernel(extra, nx, ny, rim_ref, *refs):
    refs = list(refs)
    ins, refs = refs[:extra], refs[extra:]
    halo_ref, refs = refs[0], refs[1:]
    outs, refs = refs[:extra], refs[extra:]
    land_ref, send_sem, recv_sem = refs
    gx, gy = lax.axis_index("gx"), lax.axis_index("gy")
    west, east = lax.rem(gy + ny - 1, ny), lax.rem(gy + 1, ny)
    barrier = pltpu.get_barrier_semaphore()
    mesh_id = pl.DeviceIdType.MESH
    has_north, has_south = gx > 0, gx < nx - 1

    def greet(target):
        pl.semaphore_signal(barrier, inc=1, device_id=target, device_id_type=mesh_id)

    land_ref[0] = jnp.zeros_like(land_ref[0])
    land_ref[1] = jnp.zeros_like(land_ref[1])
    greet((gx, west))
    greet((gx, east))

    @pl.when(has_north)
    def _():
        greet((gx - 1, gy))

    @pl.when(has_south)
    def _():
        greet((gx + 1, gy))

    pl.semaphore_wait(barrier, 2 + jnp.minimum(gx, 1) + jnp.minimum(nx - 1 - gx, 1))

    def copy(source, slot, target):
        return pltpu.make_async_remote_copy(
            src_ref=rim_ref.at[source],
            dst_ref=land_ref.at[slot],
            send_sem=send_sem.at[slot],
            recv_sem=recv_sem.at[slot],
            device_id=target,
            device_id_type=mesh_id,
        )

    to_south = copy(1, 0, (jnp.minimum(gx + 1, nx - 1), gy))
    to_north = copy(0, 1, (jnp.maximum(gx - 1, 0), gy))
    to_east = copy(2, 2, (gx, east))
    to_west = copy(2, 3, (gx, west))

    @pl.when(has_south)
    def _():
        to_south.start()

    @pl.when(has_north)
    def _():
        to_north.start()

    to_east.start()
    to_west.start()
    if extra:
        for k in range(3):
            outs[k][...] = ins[k][...].T
        for k in range(3, 5):
            outs[k][...] = jnp.broadcast_to(ins[k][...], outs[k].shape)
        slots, lit_ref = ins[5], outs[5]
        shape = (slots.shape[0], lit_ref.shape[2])

        def mark(r, carry):
            hit = slots[...] == lanes_of(shape) + r * shape[1]
            lit_ref[r] = jnp.max(jnp.where(hit, 1.0, 0.0), axis=0, keepdims=True)
            return carry

        lax.fori_loop(0, lit_ref.shape[0], mark, 0)

    @pl.when(has_south)
    def _():
        to_south.wait_send()

    @pl.when(has_north)
    def _():
        to_north.wait_send()

    to_east.wait()
    to_west.wait()

    @pl.when(has_north)
    def _():
        to_south.wait_recv()

    @pl.when(has_south)
    def _():
        to_north.wait_recv()

    for k in range(4):
        halo_ref[k] = land_ref[k].astype(jnp.float32)


def exchange(rim, number, ins, shapes):
    _, depth, cols = rim.shape
    nx, ny = lax.axis_size("gx"), lax.axis_size("gy")
    return pl.pallas_call(
        functools.partial(exchange_kernel, len(ins), nx, ny),
        out_shape=(jax.ShapeDtypeStruct((4, depth, cols), jnp.float32), *shapes),
        in_specs=[VMEM] * (1 + len(ins)),
        out_specs=(VMEM,) * (1 + len(shapes)),
        scratch_shapes=[
            pltpu.VMEM((4, depth, cols), jnp.bfloat16),
            pltpu.SemaphoreType.DMA((4,)),
            pltpu.SemaphoreType.DMA((4,)),
        ],
        compiler_params=pltpu.CompilerParams(collective_id=number, has_side_effects=True),
        name="exchange%d" % number,
    )(rim, *ins)


def step_kernel(
    last,
    flag_ref,
    v_ref,
    lat_ref,
    lon_ref,
    halo_ref,
    chalo_ref,
    lit_ref,
    w1_ref,
    b1_ref,
    w2_ref,
    b2_ref,
    w3_ref,
    *refs,
):
    rows, total, width = v_ref.shape
    levels = lat_ref.shape[1]
    count = total // levels
    if last:
        out_ref, src_ref, adv_ref, x_ref, one_ref, two_ref = refs
    else:
        out_ref, rim_ref, adv_ref, x_ref, one_ref, two_ref, edge_ref = refs
        edge_ref[...] = jnp.zeros_like(edge_ref)
    hidden = w1_ref.shape[0]
    lane = lanes_of((levels, width))

    def advect_row(r, slot):
        is_top = r == 0
        is_low = r == rows - 1
        up = jnp.maximum(r - 1, 0)
        down = jnp.minimum(r + 1, rows - 1)
        here = lat_ref[r]
        above = jnp.where(is_top, chalo_ref[0, chalo_ref.shape[1] - levels :, :], lat_ref[up])
        below = jnp.where(is_low, chalo_ref[1, chalo_ref.shape[1] - levels :, :], lat_ref[down])
        face0 = 0.5 * (above + here) * jnp.where(is_top, flag_ref[0], 1.0)
        face1 = 0.5 * (here + below) * jnp.where(is_low, flag_ref[1], 1.0)
        pos0, neg0 = jnp.maximum(face0, 0.0), jnp.minimum(face0, 0.0)
        pos1, neg1 = jnp.maximum(face1, 0.0), jnp.minimum(face1, 0.0)

        def west_of(value, halo):
            return jnp.where(
                lane == 0, pltpu.roll(halo, width - rows - r, axis=1), pltpu.roll(value, 1, axis=1)
            )

        def east_of(value, halo):
            return jnp.where(
                lane == width - 1,
                pltpu.roll(halo, width - 1 - r, axis=1),
                pltpu.roll(value, width - 1, axis=1),
            )

        c = lon_ref[r]
        g0 = 0.5 * (west_of(c, chalo_ref[2, chalo_ref.shape[1] - levels :, :]) + c)
        g1 = 0.5 * (c + east_of(c, chalo_ref[3, chalo_ref.shape[1] - levels :, :]))
        gpos0, gneg0 = jnp.maximum(g0, 0.0), jnp.minimum(g0, 0.0)
        gpos1, gneg1 = jnp.maximum(g1, 0.0), jnp.minimum(g1, 0.0)
        for f in range(count):
            part = slice(f * levels, (f + 1) * levels)
            v = v_ref[r, part, :]
            vn = jnp.where(is_top, halo_ref[0, part, :], v_ref[up, part, :])
            vs = jnp.where(is_low, halo_ref[1, part, :], v_ref[down, part, :])
            vw = west_of(v, halo_ref[2, part, :])
            ve = east_of(v, halo_ref[3, part, :])
            f0 = pos0 * vn + neg0 * v
            f1 = pos1 * v + neg1 * vs
            h0 = gpos0 * vw + gneg0 * v
            h1 = gpos1 * v + gneg1 * ve
            new = v - (f1 - f0) - (h1 - h0)
            adv_ref[part, slot * width : (slot + 1) * width] = new
            x_ref[part, slot * width : (slot + 1) * width] = new.astype(jnp.bfloat16)

    def body(i, carry):
        for k in range(GROUP):
            advect_row(i * GROUP + k, k)
        chunk = 256
        for h in range(0, hidden, chunk):
            acc = jnp.dot(w1_ref[h : h + chunk, :], x_ref[...], preferred_element_type=jnp.float32)
            bias = jnp.concatenate([b1_ref[h : h + chunk, :]] * GROUP, axis=1)
            one_ref[h : h + chunk, :] = silu(acc + bias).astype(jnp.bfloat16)
        for h in range(0, hidden, chunk):
            acc = jnp.dot(w2_ref[h : h + chunk, :], one_ref[...], preferred_element_type=jnp.float32)
            bias = jnp.concatenate([b2_ref[h : h + chunk, :]] * GROUP, axis=1)
            two_ref[h : h + chunk, :] = silu(acc + bias).astype(jnp.bfloat16)
        lit = jnp.concatenate([lit_ref[i * GROUP + k] for k in range(GROUP)], axis=1)
        for h in range(0, total, chunk):
            heat = jnp.dot(w3_ref[h : h + chunk, :], two_ref[...], preferred_element_type=jnp.float32)
            new = adv_ref[h : h + chunk, :] + jnp.where(lit > 0.0, heat, 0.0)
            for k in range(GROUP):
                r = i * GROUP + k
                piece = new[:, k * width : (k + 1) * width]
                if last:
                    out_ref[pl.ds(h * rows + r, chunk, stride=rows), :] = piece
                    if h >= 2 * levels:
                        src_ref[
                            h - 2 * levels : h - 2 * levels + chunk,
                            pl.ds(pl.multiple_of(r * width, width), width),
                        ] = piece.astype(jnp.bfloat16)
                else:
                    out_ref[r, h : h + chunk, :] = piece
                    at = lanes_of(piece.shape)
                    edge_ref[h : h + chunk, :] = jnp.where(
                        at == r,
                        pltpu.roll(piece, r, axis=1),
                        jnp.where(
                            at == rows + r,
                            pltpu.roll(piece, rows + 1 + r, axis=1),
                            edge_ref[h : h + chunk, :],
                        ),
                    )
        return carry

    lax.fori_loop(0, rows // GROUP, body, 0)
    if not last:
        rim_ref[0] = out_ref[0].astype(jnp.bfloat16)
        rim_ref[1] = out_ref[rows - 1].astype(jnp.bfloat16)
        rim_ref[2] = edge_ref[...].astype(jnp.bfloat16)


def step(last, flags, v, lat, lon, halo, chalo, lit, nets):
    rows, total, cols = v.shape
    levels = lat.shape[1]
    hidden = nets[0].shape[0]
    f32, bf16 = jnp.float32, jnp.bfloat16
    if last:
        outs = (
            jax.ShapeDtypeStruct((total * rows, cols), f32),
            jax.ShapeDtypeStruct((2 * levels, rows * cols), bf16),
        )
    else:
        outs = (
            jax.ShapeDtypeStruct((rows, total, cols), f32),
            jax.ShapeDtypeStruct((3, total, cols), bf16),
        )
    wide = GROUP * cols
    return pl.pallas_call(
        functools.partial(step_kernel, last),
        out_shape=outs,
        in_specs=[SMEM] + [VMEM] * 11,
        out_specs=(VMEM,) * 2,
        scratch_shapes=[
            pltpu.VMEM((total, wide), f32),
            pltpu.VMEM((total, wide), bf16),
            pltpu.VMEM((hidden, wide), bf16),
            pltpu.VMEM((hidden, wide), bf16),
        ]
        + ([] if last else [pltpu.VMEM((total, cols), f32)]),
        name="step_last" if last else "step_first",
    )(flags, v, lat, lon, halo, chalo, lit, *nets)


def pack_kernel(source_ref, target_ref, out_ref):
    tile = out_ref.shape[0]
    feats, cols = source_ref.shape
    slot = lax.broadcasted_iota(jnp.int32, (tile, cols), 0) + pl.program_id(0) * tile
    lane = lanes_of((tile, cols))
    match = slot == target_ref[...]
    for c in range(SEG):
        hit = (match & (lane % SEG == c)).astype(jnp.float32).astype(jnp.bfloat16)
        out_ref[:, c * feats : (c + 1) * feats] = lax.dot_general(
            hit, source_ref[...], (((1,), (1,)), ((), ())), preferred_element_type=jnp.float32
        ).astype(jnp.bfloat16)


def pack(source, target, slots):
    feats, cols = source.shape
    tile = 256
    return pl.pallas_call(
        pack_kernel,
        grid=(slots // tile,),
        out_shape=jax.ShapeDtypeStruct((slots, SEG * feats), jnp.bfloat16),
        in_specs=[
            pl.BlockSpec((feats, cols), lambda i: (0, 0)),
            pl.BlockSpec((1, cols), lambda i: (0, 0)),
        ],
        out_specs=pl.BlockSpec((tile, SEG * feats), lambda i: (i, 0)),
        name="pack",
    )(source, target)


def chem_kernel(arrived_ref, tag_ref, regrid_ref, w1_ref, b1_ref, w2_ref, out_ref, cell_ref):
    slots = arrived_ref.shape[0]
    feats = arrived_ref.shape[1] // SEG
    cells = out_ref.shape[0]
    segs = cells // SEG
    f32, bf16 = jnp.float32, jnp.bfloat16
    seg = lax.broadcasted_iota(jnp.int32, (segs, slots), 0) + pl.program_id(0) * segs
    pick = (seg == tag_ref[...]).astype(f32).astype(bf16)
    placed = jnp.dot(pick, arrived_ref[...], preferred_element_type=f32).astype(bf16)
    half = BLOCK // SEG
    row = lax.broadcasted_iota(jnp.int32, (BLOCK, BLOCK), 0)
    col = lax.broadcasted_iota(jnp.int32, (BLOCK, BLOCK), 1)
    order = (row == (col % half) * SEG + col // half).astype(f32).astype(bf16)
    for j in range(cells // BLOCK):
        mix = jnp.dot(regrid_ref[j], order, preferred_element_type=f32).astype(bf16)
        block = placed[j * half : (j + 1) * half, :]
        stacked = jnp.concatenate(
            [block[:, c * feats : (c + 1) * feats] for c in range(SEG)], axis=0
        )
        cell_ref[j * BLOCK : (j + 1) * BLOCK, :] = jnp.dot(
            mix, stacked, preferred_element_type=f32
        ).astype(bf16)
    hid = jnp.dot(cell_ref[...], w1_ref[...], preferred_element_type=f32) + b1_ref[...]
    out_ref[...] = jnp.dot(
        silu(hid).astype(bf16), w2_ref[...], preferred_element_type=f32
    ).astype(bf16)


def chem(arrived, tags, regrid, w1, b1, w2):
    slots, wide = arrived.shape
    feats = wide // SEG
    blocks = regrid.shape[0]
    per = 4
    hidden = w1.shape[1]
    whole = lambda *shape: pl.BlockSpec(shape, lambda i: (0,) * len(shape))
    return pl.pallas_call(
        chem_kernel,
        grid=(blocks // per,),
        out_shape=jax.ShapeDtypeStruct((blocks * BLOCK, feats), jnp.bfloat16),
        in_specs=[
            whole(slots, wide),
            whole(1, slots),
            pl.BlockSpec((per, BLOCK, BLOCK), lambda i: (i, 0, 0)),
            whole(feats, hidden),
            whole(1, hidden),
            whole(hidden, feats),
        ],
        out_specs=pl.BlockSpec((per * BLOCK, feats), lambda i: (i, 0)),
        scratch_shapes=[pltpu.VMEM((per * BLOCK, feats), jnp.bfloat16)],
        name="chem",
    )(arrived, tags, regrid, w1, b1, w2)


def local(
    fields,
    courant,
    sun_columns,
    rad_w1,
    rad_b1,
    rad_w2,
    rad_b2,
    rad_w3,
    segment_route,
    regrid_weights,
    chem_w1,
    chem_b1,
    chem_w2,
):
    field_count, levels, rows, cols = fields.shape
    columns = rows * cols
    v, lat, lon, rim = prep(fields, courant)
    place = lax.axis_index("gx")
    flags = jnp.stack([place > 0, place < lax.axis_size("gx") - 1]).astype(jnp.float32)
    bf16, f32 = jnp.bfloat16, jnp.float32
    ins = (
        rad_w1,
        rad_w2,
        rad_w3,
        rad_b1.reshape(-1, 1),
        rad_b2.reshape(-1, 1),
        sun_columns.reshape(-1, 1),
    )
    shapes = (
        *(jax.ShapeDtypeStruct(w.shape[::-1], bf16) for w in ins[:3]),
        *(jax.ShapeDtypeStruct((b.shape[0], cols), f32) for b in ins[3:5]),
        jax.ShapeDtypeStruct((rows, 1, cols), f32),
    )
    chalo, w1, w2, w3, b1, b2, lit = exchange(rim, 0, ins, shapes)
    nets = (w1, b1, w2, b2, w3)

    segment_count = columns // SEG
    tile_count = lax.axis_size("gx") * lax.axis_size("gy")
    capacity = max(2, 2 * segment_count // tile_count)
    slots = tile_count * capacity
    destination = segment_route[0].reshape(-1)
    arrival_slot = segment_route[1].reshape(-1)
    segment_index = jnp.arange(segment_count)
    same_target = (destination[None, :] == destination[:, None]) & (
        segment_index[None, :] < segment_index[:, None]
    )
    order_rank = jnp.sum(same_target.astype(jnp.int32), axis=1)
    target_row = destination * capacity + order_rank
    placement = target_row[None, :] == jnp.arange(slots)[:, None]
    slot_tags = jnp.sum(jnp.where(placement, arrival_slot[None, :] + 1, 0), axis=1) - 1
    tags = lax.all_to_all(
        slot_tags.reshape(tile_count, capacity), ("gx", "gy"), split_axis=0, concat_axis=0, tiled=True
    ).reshape(1, slots)
    column_target = jnp.repeat(target_row, SEG).reshape(1, columns)

    halo = chalo
    for repeat in range(STEPS):
        last = repeat == STEPS - 1
        v, rim = step(last, flags, v, lat, lon, halo, chalo, lit, nets)
        if not last:
            (halo,) = exchange(rim, repeat + 1, (), ())
    source = rim
    packed = pack(source, column_target, slots).reshape(tile_count, capacity, SEG * 2 * levels)
    arrived = lax.all_to_all(packed, ("gx", "gy"), split_axis=0, concat_axis=0, tiled=True)
    arrived = arrived.reshape(slots, SEG * 2 * levels)
    output = chem(arrived, tags, regrid_weights[0, 0], chem_w1, chem_b1.reshape(1, -1), chem_w2)
    return (
        v.reshape(field_count, levels, rows, cols),
        output.reshape(1, 1, columns, 2 * levels),
    )


def solution(mesh):
    return jax.shard_map(
        local,
        mesh=mesh,
        in_specs=(
            P(None, None, "gx", "gy"),
            P(None, None, "gx", "gy"),
            P("gx", "gy", None),
            P(),
            P(),
            P(),
            P(),
            P(),
            P(None, "gx", "gy", None),
            P("gx", "gy", None, None, None),
            P(),
            P(),
            P(),
        ),
        out_specs=(P(None, None, "gx", "gy"), P("gx", "gy", None, None)),
        check_vma=False,
    )
```

```python
import functools

import jax
import jax.numpy as jnp
from jax import lax
from jax.experimental import pallas as pl
from jax.experimental.pallas import tpu as pltpu
from jax.sharding import PartitionSpec as P

BLOCK = 128
SEG = 2
STEPS = 2
GROUP = 2
VMEM = pl.BlockSpec(memory_space=pltpu.VMEM)
SMEM = pl.BlockSpec(memory_space=pltpu.SMEM)


def silu(x):
    half = 0.5 * x
    return half + half * jnp.tanh(half)


def lanes_of(shape):
    return lax.broadcasted_iota(jnp.int32, shape, len(shape) - 1)


def prep_kernel(rows, f_ref, c_ref, v_ref, lat_ref, lon_ref, rim_ref, edge_ref):
    total = f_ref.shape[0] // rows
    levels = lat_ref.shape[1]
    edge_ref[...] = jnp.zeros_like(edge_ref)

    def edges(part, value, r):
        lane = lanes_of(value.shape)
        edge_ref[part, :] = jnp.where(
            lane == r,
            pltpu.roll(value, r, axis=1),
            jnp.where(
                lane == rows + r, pltpu.roll(value, rows + 1 + r, axis=1), edge_ref[part, :]
            ),
        )

    def body(r, carry):
        value = f_ref[pl.ds(r, total, stride=rows), :]
        v_ref[r] = value
        edges(slice(0, total), value, r)
        lat_ref[r] = c_ref[pl.ds(r, levels, stride=rows), :]
        lon = c_ref[pl.ds(levels * rows + r, levels, stride=rows), :]
        lon_ref[r] = lon
        edges(slice(total, total + levels), lon, r)
        return carry

    lax.fori_loop(0, rows, body, 0)
    for k, r in enumerate((0, rows - 1)):
        rim_ref[k, :total, :] = v_ref[r].astype(jnp.bfloat16)
        rim_ref[k, total:, :] = lat_ref[r].astype(jnp.bfloat16)
    rim_ref[2] = edge_ref[...].astype(jnp.bfloat16)


def prep(fields, courant):
    count, levels, rows, cols = fields.shape
    total = count * levels
    f32 = jnp.float32
    return pl.pallas_call(
        functools.partial(prep_kernel, rows),
        out_shape=(
            jax.ShapeDtypeStruct((rows, total, cols), f32),
            jax.ShapeDtypeStruct((rows, levels, cols), f32),
            jax.ShapeDtypeStruct((rows, levels, cols), f32),
            jax.ShapeDtypeStruct((3, total + levels, cols), jnp.bfloat16),
        ),
        in_specs=[VMEM, VMEM],
        out_specs=(VMEM,) * 4,
        scratch_shapes=[pltpu.VMEM((total + levels, cols), f32)],
        name="prep",
    )(fields.reshape(total * rows, cols), courant.reshape(2 * levels * rows, cols))


def exchange_kernel(extra, nx, ny, rim_ref, *refs):
    refs = list(refs)
    ins, refs = refs[:extra], refs[extra:]
    halo_ref, refs = refs[0], refs[1:]
    outs, refs = refs[:extra], refs[extra:]
    land_ref, send_sem, recv_sem = refs[:3]
    gx, gy = lax.axis_index("gx"), lax.axis_index("gy")
    west, east = lax.rem(gy + ny - 1, ny), lax.rem(gy + 1, ny)
    barrier = pltpu.get_barrier_semaphore()
    mesh_id = pl.DeviceIdType.MESH
    has_north, has_south = gx > 0, gx < nx - 1

    def greet(target):
        pl.semaphore_signal(barrier, inc=1, device_id=target, device_id_type=mesh_id)

    land_ref[0] = jnp.zeros_like(land_ref[0])
    land_ref[1] = jnp.zeros_like(land_ref[1])
    greet((gx, west))
    greet((gx, east))

    @pl.when(has_north)
    def _():
        greet((gx - 1, gy))

    @pl.when(has_south)
    def _():
        greet((gx + 1, gy))

    pl.semaphore_wait(barrier, 2 + jnp.minimum(gx, 1) + jnp.minimum(nx - 1 - gx, 1))

    def copy(source, slot, target):
        return pltpu.make_async_remote_copy(
            src_ref=rim_ref.at[source],
            dst_ref=land_ref.at[slot],
            send_sem=send_sem.at[slot],
            recv_sem=recv_sem.at[slot],
            device_id=target,
            device_id_type=mesh_id,
        )

    to_south = copy(1, 0, (jnp.minimum(gx + 1, nx - 1), gy))
    to_north = copy(0, 1, (jnp.maximum(gx - 1, 0), gy))
    to_east = copy(2, 2, (gx, east))
    to_west = copy(2, 3, (gx, west))

    @pl.when(has_south)
    def _():
        to_south.start()

    @pl.when(has_north)
    def _():
        to_north.start()

    to_east.start()
    to_west.start()
    if extra:
        for k in range(3):
            outs[k][...] = ins[k][...].T
        for k in range(3, 5):
            outs[k][...] = jnp.broadcast_to(ins[k][...], outs[k].shape[::-1]).T
        slots, lit_ref = ins[5], outs[5]
        shape = (slots.shape[1], lit_ref.shape[2])
        slot_rows = refs[3]
        slot_rows[...] = jnp.broadcast_to(slots[...], shape[::-1]).T

        def mark(r, carry):
            hit = slot_rows[...] == lanes_of(shape) + r * shape[1]
            lit_ref[r] = jnp.max(jnp.where(hit, 1.0, 0.0), axis=0, keepdims=True)
            return carry

        lax.fori_loop(0, lit_ref.shape[0], mark, 0)

    @pl.when(has_south)
    def _():
        to_south.wait_send()

    @pl.when(has_north)
    def _():
        to_north.wait_send()

    to_east.wait()
    to_west.wait()

    @pl.when(has_north)
    def _():
        to_south.wait_recv()

    @pl.when(has_south)
    def _():
        to_north.wait_recv()

    for k in range(4):
        halo_ref[k] = land_ref[k].astype(jnp.float32)


def exchange(rim, number, ins, shapes):
    _, depth, cols = rim.shape
    nx, ny = lax.axis_size("gx"), lax.axis_size("gy")
    return pl.pallas_call(
        functools.partial(exchange_kernel, len(ins), nx, ny),
        out_shape=(jax.ShapeDtypeStruct((4, depth, cols), jnp.float32), *shapes),
        in_specs=[VMEM] * (1 + len(ins)),
        out_specs=(VMEM,) * (1 + len(shapes)),
        scratch_shapes=[
            pltpu.VMEM((4, depth, cols), jnp.bfloat16),
            pltpu.SemaphoreType.DMA((4,)),
            pltpu.SemaphoreType.DMA((4,)),
        ]
        + ([pltpu.VMEM((ins[5].shape[1], cols), jnp.int32)] if ins else []),
        compiler_params=pltpu.CompilerParams(collective_id=number, has_side_effects=True),
        name="exchange%d" % number,
    )(rim, *ins)


def step_kernel(
    last,
    flag_ref,
    v_ref,
    lat_ref,
    lon_ref,
    halo_ref,
    chalo_ref,
    lit_ref,
    w1_ref,
    b1_ref,
    w2_ref,
    b2_ref,
    w3_ref,
    *refs,
):
    rows, total, width = v_ref.shape
    levels = lat_ref.shape[1]
    count = total // levels
    if last:
        out_ref, src_ref, adv_a, adv_b, x_a, x_b, one_ref, two_ref = refs
    else:
        out_ref, rim_ref, adv_a, adv_b, x_a, x_b, one_ref, two_ref, edge_ref = refs
        edge_ref[...] = jnp.zeros_like(edge_ref)
    hidden = w1_ref.shape[0]
    lane = lanes_of((levels, width))

    def advect_row(r, slot, adv_ref, x_ref):
        is_top = r == 0
        is_low = r == rows - 1
        up = jnp.maximum(r - 1, 0)
        down = jnp.minimum(r + 1, rows - 1)
        here = lat_ref[r]
        above = jnp.where(is_top, chalo_ref[0, chalo_ref.shape[1] - levels :, :], lat_ref[up])
        below = jnp.where(is_low, chalo_ref[1, chalo_ref.shape[1] - levels :, :], lat_ref[down])
        face0 = 0.5 * (above + here) * jnp.where(is_top, flag_ref[0], 1.0)
        face1 = 0.5 * (here + below) * jnp.where(is_low, flag_ref[1], 1.0)
        pos0, neg0 = jnp.maximum(face0, 0.0), jnp.minimum(face0, 0.0)
        pos1, neg1 = jnp.maximum(face1, 0.0), jnp.minimum(face1, 0.0)

        def west_of(value, halo):
            return jnp.where(
                lane == 0, pltpu.roll(halo, width - rows - r, axis=1), pltpu.roll(value, 1, axis=1)
            )

        def east_of(value, halo):
            return jnp.where(
                lane == width - 1,
                pltpu.roll(halo, width - 1 - r, axis=1),
                pltpu.roll(value, width - 1, axis=1),
            )

        c = lon_ref[r]
        g0 = 0.5 * (west_of(c, chalo_ref[2, chalo_ref.shape[1] - levels :, :]) + c)
        g1 = 0.5 * (c + east_of(c, chalo_ref[3, chalo_ref.shape[1] - levels :, :]))
        gpos0, gneg0 = jnp.maximum(g0, 0.0), jnp.minimum(g0, 0.0)
        gpos1, gneg1 = jnp.maximum(g1, 0.0), jnp.minimum(g1, 0.0)

        def one_field(f):
            part = slice(f * levels, (f + 1) * levels)
            v = v_ref[r, part, :]
            vn = jnp.where(is_top, halo_ref[0, part, :], v_ref[up, part, :])
            vs = jnp.where(is_low, halo_ref[1, part, :], v_ref[down, part, :])
            vw = west_of(v, halo_ref[2, part, :])
            ve = east_of(v, halo_ref[3, part, :])
            f0 = pos0 * vn + neg0 * v
            f1 = pos1 * v + neg1 * vs
            h0 = gpos0 * vw + gneg0 * v
            h1 = gpos1 * v + gneg1 * ve
            new = v - (f1 - f0) - (h1 - h0)
            adv_ref[part, slot * width : (slot + 1) * width] = new
            x_ref[part, slot * width : (slot + 1) * width] = new.astype(jnp.bfloat16)

        return one_field

    def advect_work(pair, adv_ref, x_ref):
        for k in range(GROUP):
            one_field = advect_row(pair * GROUP + k, k, adv_ref, x_ref)
            for f in range(count):
                one_field(f)
                yield

    def net(i, adv_ref, x_ref, work):
        chunk = 256
        for h in range(0, hidden, chunk):
            acc = jnp.dot(w1_ref[h : h + chunk, :], x_ref[...], preferred_element_type=jnp.float32)
            next(work, None)
            bias = jnp.concatenate([b1_ref[h : h + chunk, :]] * GROUP, axis=1)
            one_ref[h : h + chunk, :] = silu(acc + bias).astype(jnp.bfloat16)
        for h in range(0, hidden, chunk):
            acc = jnp.dot(w2_ref[h : h + chunk, :], one_ref[...], preferred_element_type=jnp.float32)
            next(work, None)
            bias = jnp.concatenate([b2_ref[h : h + chunk, :]] * GROUP, axis=1)
            two_ref[h : h + chunk, :] = silu(acc + bias).astype(jnp.bfloat16)
        for _ in work:
            pass
        lit = jnp.concatenate([lit_ref[i * GROUP + k] for k in range(GROUP)], axis=1)
        for h in range(0, total, chunk):
            heat = jnp.dot(w3_ref[h : h + chunk, :], two_ref[...], preferred_element_type=jnp.float32)
            new = adv_ref[h : h + chunk, :] + jnp.where(lit > 0.0, heat, 0.0)
            for k in range(GROUP):
                r = i * GROUP + k
                piece = new[:, k * width : (k + 1) * width]
                if last:
                    out_ref[pl.ds(h * rows + r, chunk, stride=rows), :] = piece
                    if h >= 2 * levels:
                        src_ref[
                            h - 2 * levels : h - 2 * levels + chunk,
                            pl.ds(pl.multiple_of(r * width, width), width),
                        ] = piece.astype(jnp.bfloat16)
                else:
                    out_ref[r, h : h + chunk, :] = piece
                    at = lanes_of(piece.shape)
                    edge_ref[h : h + chunk, :] = jnp.where(
                        at == r,
                        pltpu.roll(piece, r, axis=1),
                        jnp.where(
                            at == rows + r,
                            pltpu.roll(piece, rows + 1 + r, axis=1),
                            edge_ref[h : h + chunk, :],
                        ),
                    )

    pairs = rows // GROUP

    def body(i, carry):
        net(2 * i, adv_a, x_a, advect_work(2 * i + 1, adv_b, x_b))
        ahead = jnp.minimum(2 * i + 2, pairs - 1)
        net(2 * i + 1, adv_b, x_b, advect_work(ahead, adv_a, x_a))
        return carry

    for _ in advect_work(0, adv_a, x_a):
        pass
    lax.fori_loop(0, pairs // 2, body, 0)
    if not last:
        rim_ref[0] = out_ref[0].astype(jnp.bfloat16)
        rim_ref[1] = out_ref[rows - 1].astype(jnp.bfloat16)
        rim_ref[2] = edge_ref[...].astype(jnp.bfloat16)


def step(last, flags, v, lat, lon, halo, chalo, lit, nets):
    rows, total, cols = v.shape
    levels = lat.shape[1]
    hidden = nets[0].shape[0]
    f32, bf16 = jnp.float32, jnp.bfloat16
    if last:
        outs = (
            jax.ShapeDtypeStruct((total * rows, cols), f32),
            jax.ShapeDtypeStruct((2 * levels, rows * cols), bf16),
        )
    else:
        outs = (
            jax.ShapeDtypeStruct((rows, total, cols), f32),
            jax.ShapeDtypeStruct((3, total, cols), bf16),
        )
    wide = GROUP * cols
    return pl.pallas_call(
        functools.partial(step_kernel, last),
        out_shape=outs,
        in_specs=[SMEM] + [VMEM] * 11,
        out_specs=(VMEM,) * 2,
        scratch_shapes=[
            pltpu.VMEM((total, wide), f32),
            pltpu.VMEM((total, wide), f32),
            pltpu.VMEM((total, wide), bf16),
            pltpu.VMEM((total, wide), bf16),
            pltpu.VMEM((hidden, wide), bf16),
            pltpu.VMEM((hidden, wide), bf16),
        ]
        + ([] if last else [pltpu.VMEM((total, cols), f32)]),
        name="step_last" if last else "step_first",
    )(flags, v, lat, lon, halo, chalo, lit, *nets)


def route_kernel(
    ny, groups, source_ref, target_ref, tag_ref, out_ref, tag_out, send_ref, sems, tag_sems
):
    tiles, capacity, _ = out_ref.shape
    feats, cols = source_ref.shape
    per = tiles // groups
    me = lax.axis_index("gx") * ny + lax.axis_index("gy")
    barrier = pltpu.get_barrier_semaphore()
    mesh_id = pl.DeviceIdType.MESH

    def place(tile):
        return (lax.div(tile, ny), lax.rem(tile, ny))

    def greet(k, carry):
        pl.semaphore_signal(
            barrier, inc=1, device_id=place(lax.rem(me + k, tiles)), device_id_type=mesh_id
        )
        return carry

    lax.fori_loop(1, tiles, greet, 0)
    tile = per * capacity
    slot = lax.broadcasted_iota(jnp.int32, (tile, cols), 0)
    lane = lanes_of((1, cols))
    own = lax.div(me, per)

    def pack(j):
        group = lax.rem(own + j, groups)
        target = target_ref[...] - group * tile
        for c in range(SEG):
            wanted = jnp.where(lane % SEG == c, target, -1)
            hit = (slot == wanted).astype(jnp.float32).astype(jnp.bfloat16)
            packed = lax.dot_general(
                hit, source_ref[...], (((1,), (1,)), ((), ())), preferred_element_type=jnp.float32
            ).astype(jnp.bfloat16)
            send_ref[pl.ds(group * per, per), :, c * feats : (c + 1) * feats] = packed.reshape(
                per, capacity, feats
            )

    def copies(peer, landing):
        common = dict(device_id=place(peer), device_id_type=mesh_id)
        return (
            pltpu.make_async_remote_copy(
                src_ref=send_ref.at[peer],
                dst_ref=out_ref.at[landing],
                send_sem=sems.at[0, peer],
                recv_sem=sems.at[1, landing],
                **common,
            ),
            pltpu.make_async_remote_copy(
                src_ref=tag_ref.at[peer],
                dst_ref=tag_out.at[landing],
                send_sem=tag_sems.at[0, peer],
                recv_sem=tag_sems.at[1, landing],
                **common,
            ),
        )

    def launch(j):
        group = lax.rem(own + j, groups)
        for k in range(per):
            peer = group * per + k

            @pl.when(peer != me)
            def _():
                for copy in copies(peer, me):
                    copy.start()

    pack(groups // 2)
    pl.semaphore_wait(barrier, tiles - 1)

    def body(j, carry):
        pack(lax.rem(groups // 2 + j, groups))
        launch(lax.rem(groups // 2 + j - 1, groups))
        return carry

    lax.fori_loop(1, groups, body, 0)
    launch(groups // 2 - 1)
    out_ref[me] = send_ref[me]
    tag_out[me] = tag_ref[me]

    def finish(k, carry):
        peer = lax.rem(me + k, tiles)
        for copy in copies(peer, peer):
            copy.wait()
        return carry

    lax.fori_loop(1, tiles, finish, 0)


def route(source, target, tags):
    feats, cols = source.shape
    tiles, _, capacity = tags.shape
    bf16 = jnp.bfloat16
    return pl.pallas_call(
        functools.partial(route_kernel, lax.axis_size("gy"), 8),
        out_shape=(
            jax.ShapeDtypeStruct((tiles, capacity, SEG * feats), bf16),
            jax.ShapeDtypeStruct((tiles, 1, capacity), jnp.int32),
        ),
        in_specs=[VMEM] * 3,
        out_specs=(VMEM,) * 2,
        scratch_shapes=[
            pltpu.VMEM((tiles, capacity, SEG * feats), bf16),
            pltpu.SemaphoreType.DMA((2, tiles)),
            pltpu.SemaphoreType.DMA((2, tiles)),
        ],
        compiler_params=pltpu.CompilerParams(collective_id=7, has_side_effects=True),
        name="route",
    )(source, target, tags)


def chem_kernel(arrived_ref, tag_ref, regrid_ref, w1_ref, b1_ref, w2_ref, out_ref, cell_ref):
    slots = arrived_ref.shape[0]
    feats = arrived_ref.shape[1] // SEG
    cells = out_ref.shape[0]
    segs = cells // SEG
    f32, bf16 = jnp.float32, jnp.bfloat16
    seg = lax.broadcasted_iota(jnp.int32, (segs, slots), 0) + pl.program_id(0) * segs
    pick = (seg == tag_ref[...]).astype(f32).astype(bf16)
    placed = jnp.dot(pick, arrived_ref[...], preferred_element_type=f32).astype(bf16)
    half = BLOCK // SEG
    row = lax.broadcasted_iota(jnp.int32, (BLOCK, BLOCK), 0)
    col = lax.broadcasted_iota(jnp.int32, (BLOCK, BLOCK), 1)
    order = (row == (col % half) * SEG + col // half).astype(f32).astype(bf16)
    for j in range(cells // BLOCK):
        mix = jnp.dot(regrid_ref[j], order, preferred_element_type=f32).astype(bf16)
        block = placed[j * half : (j + 1) * half, :]
        stacked = jnp.concatenate(
            [block[:, c * feats : (c + 1) * feats] for c in range(SEG)], axis=0
        )
        cell_ref[j * BLOCK : (j + 1) * BLOCK, :] = jnp.dot(
            mix, stacked, preferred_element_type=f32
        ).astype(bf16)
    hid = jnp.dot(cell_ref[...], w1_ref[...], preferred_element_type=f32) + b1_ref[...]
    out_ref[...] = jnp.dot(
        silu(hid).astype(bf16), w2_ref[...], preferred_element_type=f32
    ).astype(bf16)


def chem(arrived, tags, regrid, w1, b1, w2):
    slots, wide = arrived.shape
    feats = wide // SEG
    blocks = regrid.shape[0]
    per = 4
    hidden = w1.shape[1]
    whole = lambda *shape: pl.BlockSpec(shape, lambda i: (0,) * len(shape))
    return pl.pallas_call(
        chem_kernel,
        grid=(blocks // per,),
        out_shape=jax.ShapeDtypeStruct((blocks * BLOCK, feats), jnp.bfloat16),
        in_specs=[
            whole(slots, wide),
            whole(1, slots),
            pl.BlockSpec((per, BLOCK, BLOCK), lambda i: (i, 0, 0)),
            whole(feats, hidden),
            whole(1, hidden),
            whole(hidden, feats),
        ],
        out_specs=pl.BlockSpec((per * BLOCK, feats), lambda i: (i, 0)),
        scratch_shapes=[pltpu.VMEM((per * BLOCK, feats), jnp.bfloat16)],
        name="chem",
    )(arrived, tags, regrid, w1, b1, w2)


def local(
    fields,
    courant,
    sun_columns,
    rad_w1,
    rad_b1,
    rad_w2,
    rad_b2,
    rad_w3,
    segment_route,
    regrid_weights,
    chem_w1,
    chem_b1,
    chem_w2,
):
    field_count, levels, rows, cols = fields.shape
    columns = rows * cols
    v, lat, lon, rim = prep(fields, courant)
    place = lax.axis_index("gx")
    flags = jnp.stack([place > 0, place < lax.axis_size("gx") - 1]).astype(jnp.float32)
    bf16, f32 = jnp.bfloat16, jnp.float32
    ins = (
        rad_w1,
        rad_w2,
        rad_w3,
        rad_b1.reshape(1, -1),
        rad_b2.reshape(1, -1),
        sun_columns.reshape(1, -1),
    )
    shapes = (
        *(jax.ShapeDtypeStruct(w.shape[::-1], bf16) for w in ins[:3]),
        *(jax.ShapeDtypeStruct((b.shape[1], cols), f32) for b in ins[3:5]),
        jax.ShapeDtypeStruct((rows, 1, cols), f32),
    )
    chalo, w1, w2, w3, b1, b2, lit = exchange(rim, 0, ins, shapes)
    nets = (w1, b1, w2, b2, w3)

    segment_count = columns // SEG
    tile_count = lax.axis_size("gx") * lax.axis_size("gy")
    capacity = max(2, 2 * segment_count // tile_count)
    slots = tile_count * capacity
    destination = segment_route[0].reshape(-1)
    arrival_slot = segment_route[1].reshape(-1)
    segment_index = jnp.arange(segment_count)
    same_target = (destination[None, :] == destination[:, None]) & (
        segment_index[None, :] < segment_index[:, None]
    )
    order_rank = jnp.sum(same_target.astype(jnp.int32), axis=1)
    target_row = destination * capacity + order_rank
    placement = target_row[None, :] == jnp.arange(slots)[:, None]
    slot_tags = jnp.sum(jnp.where(placement, arrival_slot[None, :] + 1, 0), axis=1) - 1
    slot_tags = slot_tags.reshape(tile_count, 1, capacity)
    column_target = jnp.repeat(target_row, SEG).reshape(1, columns)

    halo = chalo
    for repeat in range(STEPS):
        last = repeat == STEPS - 1
        v, rim = step(last, flags, v, lat, lon, halo, chalo, lit, nets)
        if not last:
            (halo,) = exchange(rim, repeat + 1, (), ())
    source = rim
    arrived, tags = route(source, column_target, slot_tags)
    arrived = arrived.reshape(slots, SEG * 2 * levels)
    tags = tags.reshape(1, slots)
    output = chem(arrived, tags, regrid_weights[0, 0], chem_w1, chem_b1.reshape(1, -1), chem_w2)
    return (
        v.reshape(field_count, levels, rows, cols),
        output.reshape(1, 1, columns, 2 * levels),
    )


def solution(mesh):
    return jax.shard_map(
        local,
        mesh=mesh,
        in_specs=(
            P(None, None, "gx", "gy"),
            P(None, None, "gx", "gy"),
            P("gx", "gy", None),
            P(),
            P(),
            P(),
            P(),
            P(),
            P(None, "gx", "gy", None),
            P("gx", "gy", None, None, None),
            P(),
            P(),
            P(),
        ),
        out_specs=(P(None, None, "gx", "gy"), P("gx", "gy", None, None)),
        check_vma=False,
    )
```

```python
import functools

import jax
import jax.numpy as jnp
from jax import lax
from jax.experimental import pallas as pl
from jax.experimental.pallas import tpu as pltpu
from jax.sharding import PartitionSpec as P

BLOCK = 128
SEG = 2
STEPS = 2
GROUP = 2
VMEM = pl.BlockSpec(memory_space=pltpu.VMEM)
SMEM = pl.BlockSpec(memory_space=pltpu.SMEM)


def silu(x):
    half = 0.5 * x
    return half + half * jnp.tanh(half)


def lanes_of(shape):
    return lax.broadcasted_iota(jnp.int32, shape, len(shape) - 1)


def edge_lanes(lane, r):
    width = lane.shape[-1]
    return (lane == 2 * r) | (lane == lax.rem(2 * r + width - 1, width))


def prep_kernel(rows, f_ref, c_ref, v_ref, lat_ref, lon_ref, rim_ref, edge_ref):
    total = f_ref.shape[0] // rows
    levels = lat_ref.shape[1]
    edge_ref[...] = jnp.zeros_like(edge_ref)

    def edges(part, value, r):
        lane = lanes_of(value.shape)
        edge_ref[part, :] = jnp.where(
            edge_lanes(lane, r), pltpu.roll(value, 2 * r, axis=1), edge_ref[part, :]
        )

    def body(r, carry):
        value = f_ref[pl.ds(r, total, stride=rows), :]
        v_ref[r] = value
        edges(slice(0, total), value, r)
        lat_ref[r] = c_ref[pl.ds(r, levels, stride=rows), :]
        lon = c_ref[pl.ds(levels * rows + r, levels, stride=rows), :]
        lon_ref[r] = lon
        edges(slice(total, total + levels), lon, r)
        return carry

    lax.fori_loop(0, rows, body, 0)
    for k, r in enumerate((0, rows - 1)):
        rim_ref[k, :total, :] = v_ref[r].astype(jnp.bfloat16)
        rim_ref[k, total:, :] = lat_ref[r].astype(jnp.bfloat16)
    rim_ref[2] = edge_ref[...].astype(jnp.bfloat16)


def prep(fields, courant):
    count, levels, rows, cols = fields.shape
    total = count * levels
    f32 = jnp.float32
    return pl.pallas_call(
        functools.partial(prep_kernel, rows),
        out_shape=(
            jax.ShapeDtypeStruct((rows, total, cols), f32),
            jax.ShapeDtypeStruct((rows, levels, cols), f32),
            jax.ShapeDtypeStruct((rows, levels, cols), f32),
            jax.ShapeDtypeStruct((3, total + levels, cols), jnp.bfloat16),
        ),
        in_specs=[VMEM, VMEM],
        out_specs=(VMEM,) * 4,
        scratch_shapes=[pltpu.VMEM((total + levels, cols), f32)],
        name="prep",
    )(fields.reshape(total * rows, cols), courant.reshape(2 * levels * rows, cols))


def swap_halos(nx, ny, rim_ref, land_ref, send_sem, recv_sem):
    gx, gy = lax.axis_index("gx"), lax.axis_index("gy")
    west, east = lax.rem(gy + ny - 1, ny), lax.rem(gy + 1, ny)
    barrier = pltpu.get_barrier_semaphore()
    mesh_id = pl.DeviceIdType.MESH
    has_north, has_south = gx > 0, gx < nx - 1

    def greet(target):
        pl.semaphore_signal(barrier, inc=1, device_id=target, device_id_type=mesh_id)

    def copy(source, slot, target):
        return pltpu.make_async_remote_copy(
            src_ref=rim_ref.at[source],
            dst_ref=land_ref.at[slot],
            send_sem=send_sem.at[slot],
            recv_sem=recv_sem.at[slot],
            device_id=target,
            device_id_type=mesh_id,
        )

    to_south = copy(1, 0, (jnp.minimum(gx + 1, nx - 1), gy))
    to_north = copy(0, 1, (jnp.maximum(gx - 1, 0), gy))
    to_east = copy(2, 2, (gx, east))
    to_west = copy(2, 3, (gx, west))


    def enter():
        land_ref[0] = jnp.zeros_like(land_ref[0])
        land_ref[1] = jnp.zeros_like(land_ref[1])
        greet((gx, west))
        greet((gx, east))

        @pl.when(has_north)
        def _():
            greet((gx - 1, gy))

        @pl.when(has_south)
        def _():
            greet((gx + 1, gy))

    def ready():
        pl.semaphore_wait(barrier, 2 + jnp.minimum(gx, 1) + jnp.minimum(nx - 1 - gx, 1))

    def send_rows():
        @pl.when(has_south)
        def _():
            to_south.start()

        @pl.when(has_north)
        def _():
            to_north.start()

    def send_edges():
        to_east.start()
        to_west.start()

    def finish():
        @pl.when(has_south)
        def _():
            to_south.wait_send()

        @pl.when(has_north)
        def _():
            to_north.wait_send()

        to_east.wait()
        to_west.wait()

        @pl.when(has_north)
        def _():
            to_south.wait_recv()

        @pl.when(has_south)
        def _():
            to_north.wait_recv()

    return enter, ready, send_rows, send_edges, finish


def exchange_kernel(extra, nx, ny, rim_ref, *refs):
    refs = list(refs)
    ins, refs = refs[:extra], refs[extra:]
    halo_ref, refs = refs[0], refs[1:]
    outs, refs = refs[:extra], refs[extra:]
    land_ref, send_sem, recv_sem = refs[:3]
    enter, ready, send_rows, send_edges, finish = swap_halos(
        nx, ny, rim_ref, land_ref, send_sem, recv_sem
    )
    enter()
    ready()
    send_rows()
    send_edges()
    if extra:
        for k in range(3):
            outs[k][...] = ins[k][...].T
        for k in range(3, 5):
            outs[k][...] = jnp.broadcast_to(ins[k][...], outs[k].shape[::-1]).T
        slots, lit_ref = ins[5], outs[5]
        shape = (slots.shape[1], lit_ref.shape[2])
        slot_rows = refs[3]
        slot_rows[...] = jnp.broadcast_to(slots[...], shape[::-1]).T

        def mark(r, carry):
            hit = slot_rows[...] == lanes_of(shape) + r * shape[1]
            lit_ref[r] = jnp.max(jnp.where(hit, 1.0, 0.0), axis=0, keepdims=True)
            return carry

        lax.fori_loop(0, lit_ref.shape[0], mark, 0)

    finish()
    for k in range(4):
        halo_ref[k] = land_ref[k].astype(jnp.float32)


def exchange(rim, number, ins, shapes):
    _, depth, cols = rim.shape
    nx, ny = lax.axis_size("gx"), lax.axis_size("gy")
    return pl.pallas_call(
        functools.partial(exchange_kernel, len(ins), nx, ny),
        out_shape=(jax.ShapeDtypeStruct((4, depth, cols), jnp.float32), *shapes),
        in_specs=[VMEM] * (1 + len(ins)),
        out_specs=(VMEM,) * (1 + len(shapes)),
        scratch_shapes=[
            pltpu.VMEM((4, depth, cols), jnp.bfloat16),
            pltpu.SemaphoreType.DMA((4,)),
            pltpu.SemaphoreType.DMA((4,)),
        ]
        + ([pltpu.VMEM((ins[5].shape[1], cols), jnp.int32)] if ins else []),
        compiler_params=pltpu.CompilerParams(collective_id=number, has_side_effects=True),
        name="exchange%d" % number,
    )(rim, *ins)


def step_kernel(
    last,
    nx,
    ny,
    flag_ref,
    v_ref,
    lat_ref,
    lon_ref,
    halo_ref,
    chalo_ref,
    lit_ref,
    w1_ref,
    b1_ref,
    w2_ref,
    b2_ref,
    w3_ref,
    *refs,
):
    rows, total, width = v_ref.shape
    levels = lat_ref.shape[1]
    count = total // levels
    if last:
        out_ref, src_ref, adv_a, adv_b, x_a, x_b, one_ref, two_ref = refs
    else:
        out_ref, next_ref, adv_a, adv_b, x_a, x_b, one_ref, two_ref, *refs = refs
        edge_ref, rim_ref, land_ref, send_sem, recv_sem = refs
        enter, ready, send_rows, send_edges, finish = swap_halos(
            nx, ny, rim_ref, land_ref, send_sem, recv_sem
        )
        enter()
        edge_ref[...] = jnp.zeros_like(edge_ref)
    hidden = w1_ref.shape[0]
    lane = lanes_of((levels, width))

    def advect_row(r, slot, adv_ref, x_ref):
        is_top = r == 0
        is_low = r == rows - 1
        up = jnp.maximum(r - 1, 0)
        down = jnp.minimum(r + 1, rows - 1)
        here = lat_ref[r]
        above = jnp.where(is_top, chalo_ref[0, chalo_ref.shape[1] - levels :, :], lat_ref[up])
        below = jnp.where(is_low, chalo_ref[1, chalo_ref.shape[1] - levels :, :], lat_ref[down])
        face0 = 0.5 * (above + here) * jnp.where(is_top, flag_ref[0], 1.0)
        face1 = 0.5 * (here + below) * jnp.where(is_low, flag_ref[1], 1.0)
        pos0, neg0 = jnp.maximum(face0, 0.0), jnp.minimum(face0, 0.0)
        pos1, neg1 = jnp.maximum(face1, 0.0), jnp.minimum(face1, 0.0)

        def west_of(value, halo):
            return jnp.where(
                lane == 0, pltpu.roll(halo, lax.rem(width + 1 - 2 * r, width), axis=1), pltpu.roll(value, 1, axis=1)
            )

        def east_of(value, halo):
            return jnp.where(
                lane == width - 1,
                pltpu.roll(halo, width - 1 - 2 * r, axis=1),
                pltpu.roll(value, width - 1, axis=1),
            )

        c = lon_ref[r]
        g0 = 0.5 * (west_of(c, chalo_ref[2, chalo_ref.shape[1] - levels :, :]) + c)
        g1 = 0.5 * (c + east_of(c, chalo_ref[3, chalo_ref.shape[1] - levels :, :]))
        gpos0, gneg0 = jnp.maximum(g0, 0.0), jnp.minimum(g0, 0.0)
        gpos1, gneg1 = jnp.maximum(g1, 0.0), jnp.minimum(g1, 0.0)

        def one_field(f):
            part = slice(f * levels, (f + 1) * levels)
            v = v_ref[r, part, :]
            vn = jnp.where(is_top, halo_ref[0, part, :], v_ref[up, part, :])
            vs = jnp.where(is_low, halo_ref[1, part, :], v_ref[down, part, :])
            vw = west_of(v, halo_ref[2, part, :])
            ve = east_of(v, halo_ref[3, part, :])
            f0 = pos0 * vn + neg0 * v
            f1 = pos1 * v + neg1 * vs
            h0 = gpos0 * vw + gneg0 * v
            h1 = gpos1 * v + gneg1 * ve
            new = v - (f1 - f0) - (h1 - h0)
            adv_ref[part, slot * width : (slot + 1) * width] = new
            x_ref[part, slot * width : (slot + 1) * width] = new.astype(jnp.bfloat16)

        return one_field

    def advect_work(pair, adv_ref, x_ref):
        for k in range(GROUP):
            one_field = advect_row(pair * GROUP + k, k, adv_ref, x_ref)
            for f in range(count):
                one_field(f)
                yield

    def net(i, adv_ref, x_ref, work):
        chunk = 256
        for h in range(0, hidden, chunk):
            acc = jnp.dot(w1_ref[h : h + chunk, :], x_ref[...], preferred_element_type=jnp.float32)
            next(work, None)
            bias = jnp.concatenate([b1_ref[h : h + chunk, :]] * GROUP, axis=1)
            one_ref[h : h + chunk, :] = silu(acc + bias).astype(jnp.bfloat16)
        for h in range(0, hidden, chunk):
            acc = jnp.dot(w2_ref[h : h + chunk, :], one_ref[...], preferred_element_type=jnp.float32)
            next(work, None)
            bias = jnp.concatenate([b2_ref[h : h + chunk, :]] * GROUP, axis=1)
            two_ref[h : h + chunk, :] = silu(acc + bias).astype(jnp.bfloat16)
        for _ in work:
            pass
        lit = jnp.concatenate([lit_ref[i * GROUP + k] for k in range(GROUP)], axis=1)
        for h in range(0, total, chunk):
            heat = jnp.dot(w3_ref[h : h + chunk, :], two_ref[...], preferred_element_type=jnp.float32)
            new = adv_ref[h : h + chunk, :] + jnp.where(lit > 0.0, heat, 0.0)
            for k in range(GROUP):
                r = i * GROUP + k
                piece = new[:, k * width : (k + 1) * width]
                if last:
                    out_ref[pl.ds(h * rows + r, chunk, stride=rows), :] = piece
                    if h >= 2 * levels:
                        src_ref[
                            h - 2 * levels : h - 2 * levels + chunk,
                            pl.ds(pl.multiple_of(r * width, width), width),
                        ] = piece.astype(jnp.bfloat16)
                else:
                    out_ref[r, h : h + chunk, :] = piece
                    at = lanes_of(piece.shape)
                    edge_ref[h : h + chunk, :] = jnp.where(
                        edge_lanes(at, r),
                        pltpu.roll(piece, 2 * r, axis=1),
                        edge_ref[h : h + chunk, :],
                    )

    pairs = rows // GROUP

    def order(k):
        return jnp.where(k == 0, 0, jnp.where(k == 1, pairs - 1, jnp.minimum(k - 1, pairs - 2)))

    def body(i, carry):
        net(order(2 * i), adv_a, x_a, advect_work(order(2 * i + 1), adv_b, x_b))
        net(order(2 * i + 1), adv_b, x_b, advect_work(order(2 * i + 2), adv_a, x_a))
        if not last:

            @pl.when(i == 0)
            def _():
                rim_ref[0] = out_ref[0].astype(jnp.bfloat16)
                rim_ref[1] = out_ref[rows - 1].astype(jnp.bfloat16)
                ready()
                send_rows()

        return carry

    for _ in advect_work(0, adv_a, x_a):
        pass
    lax.fori_loop(0, pairs // 2, body, 0)
    if not last:
        rim_ref[2] = edge_ref[...].astype(jnp.bfloat16)
        send_edges()
        finish()
        for k in range(4):
            next_ref[k] = land_ref[k].astype(jnp.float32)


def step(last, flags, v, lat, lon, halo, chalo, lit, nets):
    rows, total, cols = v.shape
    levels = lat.shape[1]
    hidden = nets[0].shape[0]
    f32, bf16 = jnp.float32, jnp.bfloat16
    if last:
        outs = (
            jax.ShapeDtypeStruct((total * rows, cols), f32),
            jax.ShapeDtypeStruct((2 * levels, rows * cols), bf16),
        )
    else:
        outs = (
            jax.ShapeDtypeStruct((rows, total, cols), f32),
            jax.ShapeDtypeStruct((4, total, cols), f32),
        )
    wide = GROUP * cols
    return pl.pallas_call(
        functools.partial(step_kernel, last, lax.axis_size("gx"), lax.axis_size("gy")),
        out_shape=outs,
        in_specs=[SMEM] + [VMEM] * 11,
        out_specs=(VMEM,) * 2,
        scratch_shapes=[
            pltpu.VMEM((total, wide), f32),
            pltpu.VMEM((total, wide), f32),
            pltpu.VMEM((total, wide), bf16),
            pltpu.VMEM((total, wide), bf16),
            pltpu.VMEM((hidden, wide), bf16),
            pltpu.VMEM((hidden, wide), bf16),
        ]
        + (
            []
            if last
            else [
                pltpu.VMEM((total, cols), f32),
                pltpu.VMEM((3, total, cols), bf16),
                pltpu.VMEM((4, total, cols), bf16),
                pltpu.SemaphoreType.DMA((4,)),
                pltpu.SemaphoreType.DMA((4,)),
            ]
        ),
        compiler_params=None
        if last
        else pltpu.CompilerParams(collective_id=1, has_side_effects=True),
        name="step_last" if last else "step_first",
    )(flags, v, lat, lon, halo, chalo, lit, *nets)


def route_kernel(
    ny, groups, source_ref, target_ref, tag_ref, out_ref, tag_out, send_ref, sems, tag_sems
):
    tiles, capacity, _ = out_ref.shape
    feats, cols = source_ref.shape
    per = tiles // groups
    me = lax.axis_index("gx") * ny + lax.axis_index("gy")
    barrier = pltpu.get_barrier_semaphore()
    mesh_id = pl.DeviceIdType.MESH

    def place(tile):
        return (lax.div(tile, ny), lax.rem(tile, ny))

    def greet(k, carry):
        pl.semaphore_signal(
            barrier, inc=1, device_id=place(lax.rem(me + k, tiles)), device_id_type=mesh_id
        )
        return carry

    lax.fori_loop(1, tiles, greet, 0)
    tile = per * capacity
    slot = lax.broadcasted_iota(jnp.int32, (tile, cols), 0)
    lane = lanes_of((1, cols))
    own = lax.div(me, per)

    def pack(j):
        group = lax.rem(own + j, groups)
        target = target_ref[...] - group * tile
        for c in range(SEG):
            wanted = jnp.where(lane % SEG == c, target, -1)
            hit = (slot == wanted).astype(jnp.float32).astype(jnp.bfloat16)
            packed = lax.dot_general(
                hit, source_ref[...], (((1,), (1,)), ((), ())), preferred_element_type=jnp.float32
            ).astype(jnp.bfloat16)
            send_ref[pl.ds(group * per, per), :, c * feats : (c + 1) * feats] = packed.reshape(
                per, capacity, feats
            )

    def copies(peer, landing):
        common = dict(device_id=place(peer), device_id_type=mesh_id)
        return (
            pltpu.make_async_remote_copy(
                src_ref=send_ref.at[peer],
                dst_ref=out_ref.at[landing],
                send_sem=sems.at[0, peer],
                recv_sem=sems.at[1, landing],
                **common,
            ),
            pltpu.make_async_remote_copy(
                src_ref=tag_ref.at[peer],
                dst_ref=tag_out.at[landing],
                send_sem=tag_sems.at[0, peer],
                recv_sem=tag_sems.at[1, landing],
                **common,
            ),
        )

    def launch(j):
        group = lax.rem(own + j, groups)
        for k in range(per):
            peer = group * per + k

            @pl.when(peer != me)
            def _():
                for copy in copies(peer, me):
                    copy.start()

    pack(groups // 2)
    pl.semaphore_wait(barrier, tiles - 1)

    def body(j, carry):
        pack(lax.rem(groups // 2 + j, groups))
        launch(lax.rem(groups // 2 + j - 1, groups))
        return carry

    lax.fori_loop(1, groups, body, 0)
    launch(groups // 2 - 1)
    out_ref[me] = send_ref[me]
    tag_out[me] = tag_ref[me]

    def finish(k, carry):
        peer = lax.rem(me + k, tiles)
        for copy in copies(peer, peer):
            copy.wait()
        return carry

    lax.fori_loop(1, tiles, finish, 0)


def route(source, target, tags):
    feats, cols = source.shape
    tiles, _, capacity = tags.shape
    bf16 = jnp.bfloat16
    return pl.pallas_call(
        functools.partial(route_kernel, lax.axis_size("gy"), 8),
        out_shape=(
            jax.ShapeDtypeStruct((tiles, capacity, SEG * feats), bf16),
            jax.ShapeDtypeStruct((tiles, 1, capacity), jnp.int32),
        ),
        in_specs=[VMEM] * 3,
        out_specs=(VMEM,) * 2,
        scratch_shapes=[
            pltpu.VMEM((tiles, capacity, SEG * feats), bf16),
            pltpu.SemaphoreType.DMA((2, tiles)),
            pltpu.SemaphoreType.DMA((2, tiles)),
        ],
        compiler_params=pltpu.CompilerParams(collective_id=7, has_side_effects=True),
        name="route",
    )(source, target, tags)


def chem_kernel(arrived_ref, tag_ref, regrid_ref, w1_ref, b1_ref, w2_ref, out_ref, cell_ref):
    slots = arrived_ref.shape[0]
    feats = arrived_ref.shape[1] // SEG
    cells = out_ref.shape[0]
    segs = cells // SEG
    f32, bf16 = jnp.float32, jnp.bfloat16
    seg = lax.broadcasted_iota(jnp.int32, (segs, slots), 0) + pl.program_id(0) * segs
    pick = (seg == tag_ref[...]).astype(f32).astype(bf16)
    placed = jnp.dot(pick, arrived_ref[...], preferred_element_type=f32).astype(bf16)
    half = BLOCK // SEG
    row = lax.broadcasted_iota(jnp.int32, (BLOCK, BLOCK), 0)
    col = lax.broadcasted_iota(jnp.int32, (BLOCK, BLOCK), 1)
    order = (row == (col % half) * SEG + col // half).astype(f32).astype(bf16)
    for j in range(cells // BLOCK):
        mix = jnp.dot(regrid_ref[j], order, preferred_element_type=f32).astype(bf16)
        block = placed[j * half : (j + 1) * half, :]
        stacked = jnp.concatenate(
            [block[:, c * feats : (c + 1) * feats] for c in range(SEG)], axis=0
        )
        cell_ref[j * BLOCK : (j + 1) * BLOCK, :] = jnp.dot(
            mix, stacked, preferred_element_type=f32
        ).astype(bf16)
    hid = jnp.dot(cell_ref[...], w1_ref[...], preferred_element_type=f32) + b1_ref[...]
    out_ref[...] = jnp.dot(
        silu(hid).astype(bf16), w2_ref[...], preferred_element_type=f32
    ).astype(bf16)


def chem(arrived, tags, regrid, w1, b1, w2):
    slots, wide = arrived.shape
    feats = wide // SEG
    blocks = regrid.shape[0]
    per = 4
    hidden = w1.shape[1]
    whole = lambda *shape: pl.BlockSpec(shape, lambda i: (0,) * len(shape))
    return pl.pallas_call(
        chem_kernel,
        grid=(blocks // per,),
        out_shape=jax.ShapeDtypeStruct((blocks * BLOCK, feats), jnp.bfloat16),
        in_specs=[
            whole(slots, wide),
            whole(1, slots),
            pl.BlockSpec((per, BLOCK, BLOCK), lambda i: (i, 0, 0)),
            whole(feats, hidden),
            whole(1, hidden),
            whole(hidden, feats),
        ],
        out_specs=pl.BlockSpec((per * BLOCK, feats), lambda i: (i, 0)),
        scratch_shapes=[pltpu.VMEM((per * BLOCK, feats), jnp.bfloat16)],
        name="chem",
    )(arrived, tags, regrid, w1, b1, w2)


def local(
    fields,
    courant,
    sun_columns,
    rad_w1,
    rad_b1,
    rad_w2,
    rad_b2,
    rad_w3,
    segment_route,
    regrid_weights,
    chem_w1,
    chem_b1,
    chem_w2,
):
    field_count, levels, rows, cols = fields.shape
    columns = rows * cols
    v, lat, lon, rim = prep(fields, courant)
    place = lax.axis_index("gx")
    flags = jnp.stack([place > 0, place < lax.axis_size("gx") - 1]).astype(jnp.float32)
    bf16, f32 = jnp.bfloat16, jnp.float32
    ins = (
        rad_w1,
        rad_w2,
        rad_w3,
        rad_b1.reshape(1, -1),
        rad_b2.reshape(1, -1),
        sun_columns.reshape(1, -1),
    )
    shapes = (
        *(jax.ShapeDtypeStruct(w.shape[::-1], bf16) for w in ins[:3]),
        *(jax.ShapeDtypeStruct((b.shape[1], cols), f32) for b in ins[3:5]),
        jax.ShapeDtypeStruct((rows, 1, cols), f32),
    )
    chalo, w1, w2, w3, b1, b2, lit = exchange(rim, 0, ins, shapes)
    nets = (w1, b1, w2, b2, w3)

    segment_count = columns // SEG
    tile_count = lax.axis_size("gx") * lax.axis_size("gy")
    capacity = max(2, 2 * segment_count // tile_count)
    slots = tile_count * capacity
    destination = segment_route[0].reshape(-1)
    arrival_slot = segment_route[1].reshape(-1)
    segment_index = jnp.arange(segment_count)
    same_target = (destination[None, :] == destination[:, None]) & (
        segment_index[None, :] < segment_index[:, None]
    )
    order_rank = jnp.sum(same_target.astype(jnp.int32), axis=1)
    target_row = destination * capacity + order_rank
    placement = target_row[None, :] == jnp.arange(slots)[:, None]
    slot_tags = jnp.sum(jnp.where(placement, arrival_slot[None, :] + 1, 0), axis=1) - 1
    slot_tags = slot_tags.reshape(tile_count, 1, capacity)
    column_target = jnp.repeat(target_row, SEG).reshape(1, columns)

    halo = chalo
    for repeat in range(STEPS):
        last = repeat == STEPS - 1
        v, halo = step(last, flags, v, lat, lon, halo, chalo, lit, nets)
    source = halo
    arrived, tags = route(source, column_target, slot_tags)
    arrived = arrived.reshape(slots, SEG * 2 * levels)
    tags = tags.reshape(1, slots)
    output = chem(arrived, tags, regrid_weights[0, 0], chem_w1, chem_b1.reshape(1, -1), chem_w2)
    return (
        v.reshape(field_count, levels, rows, cols),
        output.reshape(1, 1, columns, 2 * levels),
    )


def solution(mesh):
    return jax.shard_map(
        local,
        mesh=mesh,
        in_specs=(
            P(None, None, "gx", "gy"),
            P(None, None, "gx", "gy"),
            P("gx", "gy", None),
            P(),
            P(),
            P(),
            P(),
            P(),
            P(None, "gx", "gy", None),
            P("gx", "gy", None, None, None),
            P(),
            P(),
            P(),
        ),
        out_specs=(P(None, None, "gx", "gy"), P("gx", "gy", None, None)),
        check_vma=False,
    )
```

```python
import functools

import jax
import jax.numpy as jnp
from jax import lax
from jax.experimental import pallas as pl
from jax.experimental.pallas import tpu as pltpu
from jax.sharding import PartitionSpec as P

BLOCK = 128
SEG = 2
STEPS = 2
GROUP = 2
VMEM = pl.BlockSpec(memory_space=pltpu.VMEM)
SMEM = pl.BlockSpec(memory_space=pltpu.SMEM)


def silu(x):
    half = 0.5 * x
    return half + half * jnp.tanh(half)


def lanes_of(shape):
    return lax.broadcasted_iota(jnp.int32, shape, len(shape) - 1)


def edge_lanes(lane, r):
    width = lane.shape[-1]
    return (lane == 2 * r) | (lane == lax.rem(2 * r + width - 1, width))


def prep_kernel(rows, f_ref, c_ref, v_ref, lat_ref, lon_ref, rim_ref, edge_ref, send_rows):
    total = f_ref.shape[0] // rows
    levels = lat_ref.shape[1]
    for k, r in enumerate((0, rows - 1)):
        rim_ref[k, :total, :] = f_ref[pl.ds(r, total, stride=rows), :].astype(jnp.bfloat16)
        rim_ref[k, total:, :] = c_ref[pl.ds(r, levels, stride=rows), :].astype(jnp.bfloat16)
    send_rows()
    edge_ref[...] = jnp.zeros_like(edge_ref)

    def edges(part, value, r):
        lane = lanes_of(value.shape)
        edge_ref[part, :] = jnp.where(
            edge_lanes(lane, r), pltpu.roll(value, 2 * r, axis=1), edge_ref[part, :]
        )

    def body(r, carry):
        value = f_ref[pl.ds(r, total, stride=rows), :]
        v_ref[r] = value
        edges(slice(0, total), value, r)
        lat_ref[r] = c_ref[pl.ds(r, levels, stride=rows), :]
        lon = c_ref[pl.ds(levels * rows + r, levels, stride=rows), :]
        lon_ref[r] = lon
        edges(slice(total, total + levels), lon, r)
        return carry

    lax.fori_loop(0, rows, body, 0)
    rim_ref[2] = edge_ref[...].astype(jnp.bfloat16)


def swap_halos(nx, ny, rim_ref, land_ref, send_sem, recv_sem):
    gx, gy = lax.axis_index("gx"), lax.axis_index("gy")
    west, east = lax.rem(gy + ny - 1, ny), lax.rem(gy + 1, ny)
    barrier = pltpu.get_barrier_semaphore()
    mesh_id = pl.DeviceIdType.MESH
    has_north, has_south = gx > 0, gx < nx - 1

    def greet(target):
        pl.semaphore_signal(barrier, inc=1, device_id=target, device_id_type=mesh_id)

    def copy(source, slot, target):
        return pltpu.make_async_remote_copy(
            src_ref=rim_ref.at[source],
            dst_ref=land_ref.at[slot],
            send_sem=send_sem.at[slot],
            recv_sem=recv_sem.at[slot],
            device_id=target,
            device_id_type=mesh_id,
        )

    to_south = copy(1, 0, (jnp.minimum(gx + 1, nx - 1), gy))
    to_north = copy(0, 1, (jnp.maximum(gx - 1, 0), gy))
    to_east = copy(2, 2, (gx, east))
    to_west = copy(2, 3, (gx, west))


    def enter():
        land_ref[0] = jnp.zeros_like(land_ref[0])
        land_ref[1] = jnp.zeros_like(land_ref[1])
        greet((gx, west))
        greet((gx, east))

        @pl.when(has_north)
        def _():
            greet((gx - 1, gy))

        @pl.when(has_south)
        def _():
            greet((gx + 1, gy))

    def ready():
        pl.semaphore_wait(barrier, 2 + jnp.minimum(gx, 1) + jnp.minimum(nx - 1 - gx, 1))

    def send_rows():
        @pl.when(has_south)
        def _():
            to_south.start()

        @pl.when(has_north)
        def _():
            to_north.start()

    def send_edges():
        to_east.start()
        to_west.start()

    def finish():
        @pl.when(has_south)
        def _():
            to_south.wait_send()

        @pl.when(has_north)
        def _():
            to_north.wait_send()

        to_east.wait()
        to_west.wait()

        @pl.when(has_north)
        def _():
            to_south.wait_recv()

        @pl.when(has_south)
        def _():
            to_north.wait_recv()

    return enter, ready, send_rows, send_edges, finish


def exchange_kernel(rows, nx, ny, *refs):
    f_ref, c_ref, *ins = refs[:8]
    halo_ref, v_ref, lat_ref, lon_ref, *outs = refs[8:18]
    rim_ref, edge_ref, land_ref, send_sem, recv_sem, slot_rows = refs[18:]
    enter, ready, send_rows, send_edges, finish = swap_halos(
        nx, ny, rim_ref, land_ref, send_sem, recv_sem
    )
    enter()

    def first():
        ready()
        send_rows()

    prep_kernel(rows, f_ref, c_ref, v_ref, lat_ref, lon_ref, rim_ref, edge_ref, first)
    send_edges()
    for k in range(3):
        outs[k][...] = ins[k][...].T
    for k in range(3, 5):
        outs[k][...] = jnp.broadcast_to(ins[k][...], outs[k].shape[::-1]).T
    slots, lit_ref = ins[5], outs[5]
    shape = (slots.shape[1], lit_ref.shape[2])
    slot_rows[...] = jnp.broadcast_to(slots[...], shape[::-1]).T

    def mark(r, carry):
        hit = slot_rows[...] == lanes_of(shape) + r * shape[1]
        lit_ref[r] = jnp.max(jnp.where(hit, 1.0, 0.0), axis=0, keepdims=True)
        return carry

    lax.fori_loop(0, lit_ref.shape[0], mark, 0)

    finish()
    for k in range(4):
        halo_ref[k] = land_ref[k].astype(jnp.float32)


def exchange(fields, courant, ins, shapes):
    count, levels, rows, cols = fields.shape
    total = count * levels
    depth = total + levels
    nx, ny = lax.axis_size("gx"), lax.axis_size("gy")
    f32 = jnp.float32
    return pl.pallas_call(
        functools.partial(exchange_kernel, rows, nx, ny),
        out_shape=(
            jax.ShapeDtypeStruct((4, depth, cols), f32),
            jax.ShapeDtypeStruct((rows, total, cols), f32),
            jax.ShapeDtypeStruct((rows, levels, cols), f32),
            jax.ShapeDtypeStruct((rows, levels, cols), f32),
            *shapes,
        ),
        in_specs=[VMEM] * (2 + len(ins)),
        out_specs=(VMEM,) * (4 + len(shapes)),
        scratch_shapes=[
            pltpu.VMEM((3, depth, cols), jnp.bfloat16),
            pltpu.VMEM((depth, cols), f32),
            pltpu.VMEM((4, depth, cols), jnp.bfloat16),
            pltpu.SemaphoreType.DMA((4,)),
            pltpu.SemaphoreType.DMA((4,)),
            pltpu.VMEM((ins[5].shape[1], cols), jnp.int32),
        ],
        compiler_params=pltpu.CompilerParams(collective_id=0, has_side_effects=True),
        name="exchange",
    )(
        fields.reshape(total * rows, cols),
        courant.reshape(2 * levels * rows, cols),
        *ins,
    )


def step_kernel(
    last,
    nx,
    ny,
    flag_ref,
    v_ref,
    lat_ref,
    lon_ref,
    halo_ref,
    chalo_ref,
    lit_ref,
    w1_ref,
    b1_ref,
    w2_ref,
    b2_ref,
    w3_ref,
    *refs,
):
    rows, total, width = v_ref.shape
    levels = lat_ref.shape[1]
    count = total // levels
    if last:
        out_ref, src_ref, adv_a, adv_b, x_a, x_b, one_ref, two_ref = refs
    else:
        out_ref, next_ref, adv_a, adv_b, x_a, x_b, one_ref, two_ref, *refs = refs
        edge_ref, rim_ref, land_ref, send_sem, recv_sem = refs
        enter, ready, send_rows, send_edges, finish = swap_halos(
            nx, ny, rim_ref, land_ref, send_sem, recv_sem
        )
        enter()
        edge_ref[...] = jnp.zeros_like(edge_ref)
    hidden = w1_ref.shape[0]
    lane = lanes_of((levels, width))

    def advect_row(r, slot, adv_ref, x_ref):
        is_top = r == 0
        is_low = r == rows - 1
        up = jnp.maximum(r - 1, 0)
        down = jnp.minimum(r + 1, rows - 1)
        here = lat_ref[r]
        above = jnp.where(is_top, chalo_ref[0, chalo_ref.shape[1] - levels :, :], lat_ref[up])
        below = jnp.where(is_low, chalo_ref[1, chalo_ref.shape[1] - levels :, :], lat_ref[down])
        face0 = 0.5 * (above + here) * jnp.where(is_top, flag_ref[0], 1.0)
        face1 = 0.5 * (here + below) * jnp.where(is_low, flag_ref[1], 1.0)
        pos0, neg0 = jnp.maximum(face0, 0.0), jnp.minimum(face0, 0.0)
        pos1, neg1 = jnp.maximum(face1, 0.0), jnp.minimum(face1, 0.0)

        def west_of(value, halo):
            return jnp.where(
                lane == 0, pltpu.roll(halo, lax.rem(width + 1 - 2 * r, width), axis=1), pltpu.roll(value, 1, axis=1)
            )

        def east_of(value, halo):
            return jnp.where(
                lane == width - 1,
                pltpu.roll(halo, width - 1 - 2 * r, axis=1),
                pltpu.roll(value, width - 1, axis=1),
            )

        c = lon_ref[r]
        g0 = 0.5 * (west_of(c, chalo_ref[2, chalo_ref.shape[1] - levels :, :]) + c)
        g1 = 0.5 * (c + east_of(c, chalo_ref[3, chalo_ref.shape[1] - levels :, :]))
        gpos0, gneg0 = jnp.maximum(g0, 0.0), jnp.minimum(g0, 0.0)
        gpos1, gneg1 = jnp.maximum(g1, 0.0), jnp.minimum(g1, 0.0)

        def one_field(f):
            part = slice(f * levels, (f + 1) * levels)
            v = v_ref[r, part, :]
            vn = jnp.where(is_top, halo_ref[0, part, :], v_ref[up, part, :])
            vs = jnp.where(is_low, halo_ref[1, part, :], v_ref[down, part, :])
            vw = west_of(v, halo_ref[2, part, :])
            ve = east_of(v, halo_ref[3, part, :])
            f0 = pos0 * vn + neg0 * v
            f1 = pos1 * v + neg1 * vs
            h0 = gpos0 * vw + gneg0 * v
            h1 = gpos1 * v + gneg1 * ve
            new = v - (f1 - f0) - (h1 - h0)
            adv_ref[part, slot * width : (slot + 1) * width] = new
            x_ref[part, slot * width : (slot + 1) * width] = new.astype(jnp.bfloat16)

        return one_field

    def advect_work(pair, adv_ref, x_ref):
        for k in range(GROUP):
            one_field = advect_row(pair * GROUP + k, k, adv_ref, x_ref)
            for f in range(count):
                one_field(f)
                yield

    def net(i, adv_ref, x_ref, work):
        chunk = 256
        for h in range(0, hidden, chunk):
            acc = jnp.dot(w1_ref[h : h + chunk, :], x_ref[...], preferred_element_type=jnp.float32)
            next(work, None)
            bias = jnp.concatenate([b1_ref[h : h + chunk, :]] * GROUP, axis=1)
            one_ref[h : h + chunk, :] = silu(acc + bias).astype(jnp.bfloat16)
        for h in range(0, hidden, chunk):
            acc = jnp.dot(w2_ref[h : h + chunk, :], one_ref[...], preferred_element_type=jnp.float32)
            next(work, None)
            bias = jnp.concatenate([b2_ref[h : h + chunk, :]] * GROUP, axis=1)
            two_ref[h : h + chunk, :] = silu(acc + bias).astype(jnp.bfloat16)
        for _ in work:
            pass
        lit = jnp.concatenate([lit_ref[i * GROUP + k] for k in range(GROUP)], axis=1)
        for h in range(0, total, chunk):
            heat = jnp.dot(w3_ref[h : h + chunk, :], two_ref[...], preferred_element_type=jnp.float32)
            new = adv_ref[h : h + chunk, :] + jnp.where(lit > 0.0, heat, 0.0)
            for k in range(GROUP):
                r = i * GROUP + k
                piece = new[:, k * width : (k + 1) * width]
                if last:
                    out_ref[pl.ds(h * rows + r, chunk, stride=rows), :] = piece
                    if h >= 2 * levels:
                        src_ref[
                            h - 2 * levels : h - 2 * levels + chunk,
                            pl.ds(pl.multiple_of(r * width, width), width),
                        ] = piece.astype(jnp.bfloat16)
                else:
                    out_ref[r, h : h + chunk, :] = piece
                    at = lanes_of(piece.shape)
                    edge_ref[h : h + chunk, :] = jnp.where(
                        edge_lanes(at, r),
                        pltpu.roll(piece, 2 * r, axis=1),
                        edge_ref[h : h + chunk, :],
                    )

    pairs = rows // GROUP

    def order(k):
        return jnp.where(k == 0, 0, jnp.where(k == 1, pairs - 1, jnp.minimum(k - 1, pairs - 2)))

    def body(i, carry):
        net(order(2 * i), adv_a, x_a, advect_work(order(2 * i + 1), adv_b, x_b))
        net(order(2 * i + 1), adv_b, x_b, advect_work(order(2 * i + 2), adv_a, x_a))
        if not last:

            @pl.when(i == 0)
            def _():
                rim_ref[0] = out_ref[0].astype(jnp.bfloat16)
                rim_ref[1] = out_ref[rows - 1].astype(jnp.bfloat16)
                ready()
                send_rows()

        return carry

    for _ in advect_work(0, adv_a, x_a):
        pass
    lax.fori_loop(0, pairs // 2, body, 0)
    if not last:
        rim_ref[2] = edge_ref[...].astype(jnp.bfloat16)
        send_edges()
        finish()
        for k in range(4):
            next_ref[k] = land_ref[k].astype(jnp.float32)


def step(last, flags, v, lat, lon, halo, chalo, lit, nets):
    rows, total, cols = v.shape
    levels = lat.shape[1]
    hidden = nets[0].shape[0]
    f32, bf16 = jnp.float32, jnp.bfloat16
    if last:
        outs = (
            jax.ShapeDtypeStruct((total * rows, cols), f32),
            jax.ShapeDtypeStruct((2 * levels, rows * cols), bf16),
        )
    else:
        outs = (
            jax.ShapeDtypeStruct((rows, total, cols), f32),
            jax.ShapeDtypeStruct((4, total, cols), f32),
        )
    wide = GROUP * cols
    return pl.pallas_call(
        functools.partial(step_kernel, last, lax.axis_size("gx"), lax.axis_size("gy")),
        out_shape=outs,
        in_specs=[SMEM] + [VMEM] * 11,
        out_specs=(VMEM,) * 2,
        scratch_shapes=[
            pltpu.VMEM((total, wide), f32),
            pltpu.VMEM((total, wide), f32),
            pltpu.VMEM((total, wide), bf16),
            pltpu.VMEM((total, wide), bf16),
            pltpu.VMEM((hidden, wide), bf16),
            pltpu.VMEM((hidden, wide), bf16),
        ]
        + (
            []
            if last
            else [
                pltpu.VMEM((total, cols), f32),
                pltpu.VMEM((3, total, cols), bf16),
                pltpu.VMEM((4, total, cols), bf16),
                pltpu.SemaphoreType.DMA((4,)),
                pltpu.SemaphoreType.DMA((4,)),
            ]
        ),
        compiler_params=None
        if last
        else pltpu.CompilerParams(collective_id=1, has_side_effects=True),
        name="step_last" if last else "step_first",
    )(flags, v, lat, lon, halo, chalo, lit, *nets)


def route_kernel(
    ny, groups, source_ref, target_ref, tag_ref, out_ref, tag_out, send_ref, sems, tag_sems
):
    tiles, capacity, _ = out_ref.shape
    feats, cols = source_ref.shape
    per = tiles // groups
    me = lax.axis_index("gx") * ny + lax.axis_index("gy")
    barrier = pltpu.get_barrier_semaphore()
    mesh_id = pl.DeviceIdType.MESH

    def place(tile):
        return (lax.div(tile, ny), lax.rem(tile, ny))

    def greet(k, carry):
        pl.semaphore_signal(
            barrier, inc=1, device_id=place(lax.rem(me + k, tiles)), device_id_type=mesh_id
        )
        return carry

    lax.fori_loop(1, tiles, greet, 0)
    tile = per * capacity
    slot = lax.broadcasted_iota(jnp.int32, (tile, cols), 0)
    lane = lanes_of((1, cols))
    own = lax.div(me, per)

    def pack(j):
        group = lax.rem(own + j, groups)
        target = target_ref[...] - group * tile
        for c in range(SEG):
            wanted = jnp.where(lane % SEG == c, target, -1)
            hit = (slot == wanted).astype(jnp.float32).astype(jnp.bfloat16)
            packed = lax.dot_general(
                hit, source_ref[...], (((1,), (1,)), ((), ())), preferred_element_type=jnp.float32
            ).astype(jnp.bfloat16)
            send_ref[pl.ds(group * per, per), :, c * feats : (c + 1) * feats] = packed.reshape(
                per, capacity, feats
            )

    def copies(peer, landing):
        common = dict(device_id=place(peer), device_id_type=mesh_id)
        return (
            pltpu.make_async_remote_copy(
                src_ref=send_ref.at[peer],
                dst_ref=out_ref.at[landing],
                send_sem=sems.at[0, peer],
                recv_sem=sems.at[1, landing],
                **common,
            ),
            pltpu.make_async_remote_copy(
                src_ref=tag_ref.at[peer],
                dst_ref=tag_out.at[landing],
                send_sem=tag_sems.at[0, peer],
                recv_sem=tag_sems.at[1, landing],
                **common,
            ),
        )

    def launch(j):
        group = lax.rem(own + j, groups)
        for k in range(per):
            peer = group * per + k

            @pl.when(peer != me)
            def _():
                for copy in copies(peer, me):
                    copy.start()

    pack(groups // 2)
    pl.semaphore_wait(barrier, tiles - 1)

    def body(j, carry):
        pack(lax.rem(groups // 2 + j, groups))
        launch(lax.rem(groups // 2 + j - 1, groups))
        return carry

    lax.fori_loop(1, groups, body, 0)
    launch(groups // 2 - 1)
    out_ref[me] = send_ref[me]
    tag_out[me] = tag_ref[me]

    def finish(k, carry):
        peer = lax.rem(me + k, tiles)
        for copy in copies(peer, peer):
            copy.wait()
        return carry

    lax.fori_loop(1, tiles, finish, 0)


def route(source, target, tags):
    feats, cols = source.shape
    tiles, _, capacity = tags.shape
    bf16 = jnp.bfloat16
    return pl.pallas_call(
        functools.partial(route_kernel, lax.axis_size("gy"), 8),
        out_shape=(
            jax.ShapeDtypeStruct((tiles, capacity, SEG * feats), bf16),
            jax.ShapeDtypeStruct((tiles, 1, capacity), jnp.int32),
        ),
        in_specs=[VMEM] * 3,
        out_specs=(VMEM,) * 2,
        scratch_shapes=[
            pltpu.VMEM((tiles, capacity, SEG * feats), bf16),
            pltpu.SemaphoreType.DMA((2, tiles)),
            pltpu.SemaphoreType.DMA((2, tiles)),
        ],
        compiler_params=pltpu.CompilerParams(collective_id=7, has_side_effects=True),
        name="route",
    )(source, target, tags)


def chem_kernel(arrived_ref, tag_ref, regrid_ref, w1_ref, b1_ref, w2_ref, out_ref, cell_ref):
    slots = arrived_ref.shape[0]
    feats = arrived_ref.shape[1] // SEG
    cells = out_ref.shape[0]
    segs = cells // SEG
    f32, bf16 = jnp.float32, jnp.bfloat16
    seg = lax.broadcasted_iota(jnp.int32, (segs, slots), 0) + pl.program_id(0) * segs
    pick = (seg == tag_ref[...]).astype(f32).astype(bf16)
    placed = jnp.dot(pick, arrived_ref[...], preferred_element_type=f32).astype(bf16)
    half = BLOCK // SEG
    row = lax.broadcasted_iota(jnp.int32, (BLOCK, BLOCK), 0)
    col = lax.broadcasted_iota(jnp.int32, (BLOCK, BLOCK), 1)
    order = (row == (col % half) * SEG + col // half).astype(f32).astype(bf16)
    for j in range(cells // BLOCK):
        mix = jnp.dot(regrid_ref[j], order, preferred_element_type=f32).astype(bf16)
        block = placed[j * half : (j + 1) * half, :]
        stacked = jnp.concatenate(
            [block[:, c * feats : (c + 1) * feats] for c in range(SEG)], axis=0
        )
        cell_ref[j * BLOCK : (j + 1) * BLOCK, :] = jnp.dot(
            mix, stacked, preferred_element_type=f32
        ).astype(bf16)
    hid = jnp.dot(cell_ref[...], w1_ref[...], preferred_element_type=f32) + b1_ref[...]
    out_ref[...] = jnp.dot(
        silu(hid).astype(bf16), w2_ref[...], preferred_element_type=f32
    ).astype(bf16)


def chem(arrived, tags, regrid, w1, b1, w2):
    slots, wide = arrived.shape
    feats = wide // SEG
    blocks = regrid.shape[0]
    per = 4
    hidden = w1.shape[1]
    whole = lambda *shape: pl.BlockSpec(shape, lambda i: (0,) * len(shape))
    return pl.pallas_call(
        chem_kernel,
        grid=(blocks // per,),
        out_shape=jax.ShapeDtypeStruct((blocks * BLOCK, feats), jnp.bfloat16),
        in_specs=[
            whole(slots, wide),
            whole(1, slots),
            pl.BlockSpec((per, BLOCK, BLOCK), lambda i: (i, 0, 0)),
            whole(feats, hidden),
            whole(1, hidden),
            whole(hidden, feats),
        ],
        out_specs=pl.BlockSpec((per * BLOCK, feats), lambda i: (i, 0)),
        scratch_shapes=[pltpu.VMEM((per * BLOCK, feats), jnp.bfloat16)],
        name="chem",
    )(arrived, tags, regrid, w1, b1, w2)


def local(
    fields,
    courant,
    sun_columns,
    rad_w1,
    rad_b1,
    rad_w2,
    rad_b2,
    rad_w3,
    segment_route,
    regrid_weights,
    chem_w1,
    chem_b1,
    chem_w2,
):
    field_count, levels, rows, cols = fields.shape
    columns = rows * cols
    place = lax.axis_index("gx")
    flags = jnp.stack([place > 0, place < lax.axis_size("gx") - 1]).astype(jnp.float32)
    bf16, f32 = jnp.bfloat16, jnp.float32
    ins = (
        rad_w1,
        rad_w2,
        rad_w3,
        rad_b1.reshape(1, -1),
        rad_b2.reshape(1, -1),
        sun_columns.reshape(1, -1),
    )
    shapes = (
        *(jax.ShapeDtypeStruct(w.shape[::-1], bf16) for w in ins[:3]),
        *(jax.ShapeDtypeStruct((b.shape[1], cols), f32) for b in ins[3:5]),
        jax.ShapeDtypeStruct((rows, 1, cols), f32),
    )
    chalo, v, lat, lon, w1, w2, w3, b1, b2, lit = exchange(fields, courant, ins, shapes)
    nets = (w1, b1, w2, b2, w3)

    segment_count = columns // SEG
    tile_count = lax.axis_size("gx") * lax.axis_size("gy")
    capacity = max(2, 2 * segment_count // tile_count)
    slots = tile_count * capacity
    destination = segment_route[0].reshape(-1)
    arrival_slot = segment_route[1].reshape(-1)
    segment_index = jnp.arange(segment_count)
    same_target = (destination[None, :] == destination[:, None]) & (
        segment_index[None, :] < segment_index[:, None]
    )
    order_rank = jnp.sum(same_target.astype(jnp.int32), axis=1)
    target_row = destination * capacity + order_rank
    placement = target_row[None, :] == jnp.arange(slots)[:, None]
    slot_tags = jnp.sum(jnp.where(placement, arrival_slot[None, :] + 1, 0), axis=1) - 1
    slot_tags = slot_tags.reshape(tile_count, 1, capacity)
    column_target = jnp.repeat(target_row, SEG).reshape(1, columns)

    halo = chalo
    for repeat in range(STEPS):
        last = repeat == STEPS - 1
        v, halo = step(last, flags, v, lat, lon, halo, chalo, lit, nets)
    source = halo
    arrived, tags = route(source, column_target, slot_tags)
    arrived = arrived.reshape(slots, SEG * 2 * levels)
    tags = tags.reshape(1, slots)
    output = chem(arrived, tags, regrid_weights[0, 0], chem_w1, chem_b1.reshape(1, -1), chem_w2)
    return (
        v.reshape(field_count, levels, rows, cols),
        output.reshape(1, 1, columns, 2 * levels),
    )


def solution(mesh):
    return jax.shard_map(
        local,
        mesh=mesh,
        in_specs=(
            P(None, None, "gx", "gy"),
            P(None, None, "gx", "gy"),
            P("gx", "gy", None),
            P(),
            P(),
            P(),
            P(),
            P(),
            P(None, "gx", "gy", None),
            P("gx", "gy", None, None, None),
            P(),
            P(),
            P(),
        ),
        out_specs=(P(None, None, "gx", "gy"), P("gx", "gy", None, None)),
        check_vma=False,
    )
```
